768 devices in a mesh: grp: 4 (over x), gx: 48 (over y_hi, z), gy: 4 (over y_lo, core).
Axes of the slice: x: 4, y: 8 (y_hi: 4, y_lo: 2; y = y_hi * 2 + y_lo), z: 12, core: 2. Of those that a mesh axis runs over, the one named last changes fastest.
Arguments:
- potential_thermal_anomaly: float32 [192, 192, 128], P('gx', 'grp', 'gy'), may hold values from -6 to 6
- saltiness_anomaly: float32 [192, 192, 128], P('gx', 'grp', 'gy'), may hold values from -6 to 6
- x_boundary_transport_speed: float32 [192, 192, 128], P('gx', 'grp', 'gy'), may hold values from -1.8 to 1.8
- y_boundary_transport_speed: float32 [192, 192, 128], P('gx', 'grp', 'gy'), may hold values from -1.8 to 1.8
- solute_concentrations: float32 [192, 192, 17, 128], P('gx', ('grp', 'gy')), may hold values from 0.05 to 2
- ocean_site_indicator: int32 [192, 192], P('gx', 'grp'), may hold values 0 or 1
- flooded_layer_number: int32 [192, 192], P('gx', 'grp'), may hold values from 1 to 128
Outputs:
- temperature_out: float32 [192, 192, 128], P('gx', 'grp', 'gy')
- salinity_out: float32 [192, 192, 128], P('gx', 'grp', 'gy')
- east_out: float32 [192, 192, 128], P('gx', 'grp', 'gy')
- north_out: float32 [192, 192, 128], P('gx', 'grp', 'gy')
- tracers_out: float32 [192, 192, 17, 128], P('gx', ('grp', 'gy'))
The draws below stay inside these ranges and needn't reach their ends.
All inputs are finite; a program needn't handle non-finite values. No bound on the sum of `ocean_site_indicator` on one device may be relied on, other than what follows from the above.
Results may differ from the reference program's by a relative error of at most 0.0065.
Values sent between devices are 32-bit elements; how exact they have to be, the bound alone decides.
No kernel may reach another device: no remote copies, remote signals or barrier semaphores. Data moves between devices by JAX's collectives and lax.ppermute only.
A program may use at most 32 MiB of HBM per device.

```python
import math
import jax
import jax.numpy as jnp
from jax import lax

GROUP_SPAN = 4
VERTICAL_LAYERS = 128
NTR = 17
STEPS = 2
LONGITUDE_LINES = 192
LATITUDE_LINES = 192


def with_ends(entries, rng, smallest, high):
    longest = entries.shape.index(max(entries.shape))
    spots = []
    for shift in (0, 1):
        where = [jax.random.randint(jax.random.fold_in(rng, axis), (), 0, length) for axis, length in enumerate(entries.shape)]
        where[longest] = (where[longest] + shift) % entries.shape[longest]
        spots.append(tuple(where))
    return entries.at[spots[0]].set(smallest).at[spots[1]].set(high)


def block_levels(own_key, dims, split, least, top_value):
    def one(dim, parts):
        steps = jax.random.uniform(jax.random.fold_in(jax.random.fold_in(own_key, 6), dim), (parts,), jnp.float32, least / len(split), top_value / len(split))
        return jnp.repeat(jnp.exp(steps), dims[dim] // parts).reshape((-1,) + (1,) * (len(dims) - dim - 1))

    level = one(*split[0])
    for cut in split[1:]:
        level = level * one(*cut)
    return level


def centred(key, dims, deviation, most, split=(), kind=jnp.bfloat16):
    drawn = deviation * jax.random.normal(key, dims, jnp.float32)
    if split:
        drawn = drawn * block_levels(key, dims, split, -0.22, 0.18)
    return jnp.clip(drawn, -most, most).astype(kind)


def setup_inputs(seed: int = 0) -> dict:
    arg_keys = jax.random.split(jax.random.key(seed), 8)
    return {
        "potential_thermal_anomaly": centred(arg_keys[0], (LONGITUDE_LINES, LATITUDE_LINES, VERTICAL_LAYERS), 1.0, 6.0, ((0, 48), (1, 4), (2, 4)), jnp.float32),
        "saltiness_anomaly": centred(arg_keys[1], (LONGITUDE_LINES, LATITUDE_LINES, VERTICAL_LAYERS), 1.0, 6.0, ((0, 48), (1, 4), (2, 4)), jnp.float32),
        "x_boundary_transport_speed": centred(arg_keys[2], (LONGITUDE_LINES, LATITUDE_LINES, VERTICAL_LAYERS), 0.3, 1.8, ((0, 48), (1, 4), (2, 4)), jnp.float32),
        "y_boundary_transport_speed": centred(arg_keys[3], (LONGITUDE_LINES, LATITUDE_LINES, VERTICAL_LAYERS), 0.3, 1.8, ((0, 48), (1, 4), (2, 4)), jnp.float32),
        "solute_concentrations": jnp.clip(jnp.exp(math.log(2.0) - 3.6888794 * jax.random.uniform(arg_keys[4], (LONGITUDE_LINES, LATITUDE_LINES, NTR, VERTICAL_LAYERS), jnp.float32) ** block_levels(arg_keys[4], (LONGITUDE_LINES, LATITUDE_LINES, NTR, VERTICAL_LAYERS), ((0, 48), (1, 16)), -0.2, 0.2)), 0.05, 2.0),
        "ocean_site_indicator": with_ends((jax.random.randint(arg_keys[5], (LONGITUDE_LINES, LATITUDE_LINES), 0, 5) < 4).astype(jnp.int32), jax.random.fold_in(arg_keys[5], 1), 0, 1),
        "flooded_layer_number": with_ends(jax.random.randint(arg_keys[6], (LONGITUDE_LINES, LATITUDE_LINES), 1, VERTICAL_LAYERS + 1), jax.random.fold_in(arg_keys[6], 1), 1, VERTICAL_LAYERS).astype(jnp.int32),
    }


ADV_STEP = 0.1
DIFFUSION = 0.1
TURN_COS = 0.955336489125606
TURN_SIN = 0.29552020666134
PRESSURE = 0.2
HALINE = 0.8
BIO_STEP = 0.5
WATER_ATT = 0.005
CHLORO_ATT = 0.003
HEATING = 20.0
TEMP_RATE = 0.0633
NUTRIENT_HALF = 0.5
PREY_HALF = 0.5
GRAZING = 0.8
PHYTO_LOSS = 0.1
GRAZER_LOSS = 0.15
ASSIMILATE = 0.3


def limiter(first, second):
    return jnp.where(first * second > 0, jnp.where(jnp.abs(first) < jnp.abs(second), first, second), 0.0)


def advect(tracer, east_flow, north_flow):
    along_x = tracer[:, 2:-2]
    count_x = along_x.shape[0] - 4
    diff_x = along_x[1:] - along_x[:-1]
    slope_x = limiter(diff_x[:-1], diff_x[1:])
    left_x = along_x[1:count_x + 2] + 0.5 * slope_x[0:count_x + 1]
    right_x = along_x[2:count_x + 3] - 0.5 * slope_x[1:count_x + 2]
    face_x = east_flow[0:count_x + 1, 1:-1][:, :, None, :]
    flux_x = jnp.maximum(face_x, 0.0) * left_x + jnp.minimum(face_x, 0.0) * right_x
    along_y = tracer[2:-2]
    count_y = along_y.shape[1] - 4
    diff_y = along_y[:, 1:] - along_y[:, :-1]
    slope_y = limiter(diff_y[:, :-1], diff_y[:, 1:])
    left_y = along_y[:, 1:count_y + 2] + 0.5 * slope_y[:, 0:count_y + 1]
    right_y = along_y[:, 2:count_y + 3] - 0.5 * slope_y[:, 1:count_y + 2]
    face_y = north_flow[1:-1, 0:count_y + 1][:, :, None, :]
    flux_y = jnp.maximum(face_y, 0.0) * left_y + jnp.minimum(face_y, 0.0) * right_y
    centre = tracer[2:-2, 2:-2]
    return centre - ADV_STEP * ((flux_x[1:] - flux_x[:-1]) + (flux_y[:, 1:] - flux_y[:, :-1]))


def react(tracer, temper, wetness):
    depth = tracer.shape[-1]
    upper_rows = lax.broadcasted_iota(jnp.int32, (depth, depth), 0)
    upper_cols = lax.broadcasted_iota(jnp.int32, (depth, depth), 1)
    upper = jnp.where(upper_rows < upper_cols, 1.0, jnp.where(upper_rows == upper_cols, 0.5, 0.0)).astype(jnp.float32)
    classes = jnp.arange(8, dtype=jnp.float32)
    theta = (0.3 + 0.1 * classes)[:, None]
    growth_rate = (0.6 + 0.15 * classes)[:, None]
    light_half = (0.1 + 0.1 * classes)[:, None]
    nutrient = tracer[:, :, 0]
    phyto = tracer[:, :, 1:9]
    grazer = tracer[:, :, 9:17]
    chloro = jnp.sum(theta * phyto, axis=2)
    absorb = WATER_ATT + CHLORO_ATT * jnp.abs(chloro)
    optical = jnp.dot(absorb, upper, precision=lax.Precision.HIGHEST, preferred_element_type=jnp.float32)
    light = jnp.exp(-optical)
    thermal_energy_sum = HEATING * absorb * light * wetness
    warm = jnp.exp(TEMP_RATE * temper)
    limit = nutrient / (jnp.abs(nutrient) + NUTRIENT_HALF)
    lit = light[:, :, None]
    growth = growth_rate * (warm * limit)[:, :, None] * lit / (lit + light_half) * phyto
    grazed = GRAZING * grazer * phyto / (jnp.abs(phyto) + PREY_HALF)
    new_phyto = phyto + BIO_STEP * (growth - grazed - PHYTO_LOSS * phyto)
    new_grazer = grazer + BIO_STEP * (ASSIMILATE * grazed - GRAZER_LOSS * grazer)
    new_nutrient = nutrient + BIO_STEP * (-jnp.sum(growth, axis=2) + PHYTO_LOSS * jnp.sum(phyto, axis=2)
                                          + GRAZER_LOSS * jnp.sum(grazer, axis=2) + (1.0 - ASSIMILATE) * jnp.sum(grazed, axis=2))
    result = jnp.concatenate([new_nutrient[:, :, None], new_phyto, new_grazer], axis=2) * wetness[:, :, None]
    return result, thermal_energy_sum


def dynamics_update(temp_rim, salt_rim, flooded_edge_indicator, east_flow, north_flow):
    wet_mid = flooded_edge_indicator[1:-1, 1:-1]
    open_east = wet_mid * flooded_edge_indicator[2:, 1:-1]
    open_west = flooded_edge_indicator[:-2, 1:-1] * wet_mid
    open_north = wet_mid * flooded_edge_indicator[1:-1, 2:]
    open_south = flooded_edge_indicator[1:-1, :-2] * wet_mid

    def laplace(field):
        middle = field[1:-1, 1:-1]
        return (open_east * (field[2:, 1:-1] - middle) - open_west * (middle - field[:-2, 1:-1])
                + open_north * (field[1:-1, 2:] - middle) - open_south * (middle - field[1:-1, :-2]))

    buoyancy = temp_rim - HALINE * salt_rim
    buoy_mid = buoyancy[1:-1, 1:-1]
    new_temp = wet_mid * (temp_rim[1:-1, 1:-1] + DIFFUSION * laplace(temp_rim))
    new_salt = wet_mid * (salt_rim[1:-1, 1:-1] + DIFFUSION * laplace(salt_rim))
    new_east = open_east * (TURN_COS * east_flow + TURN_SIN * north_flow - PRESSURE * (buoyancy[2:, 1:-1] - buoy_mid))
    new_north = open_north * (-TURN_SIN * east_flow + TURN_COS * north_flow - PRESSURE * (buoyancy[1:-1, 2:] - buoy_mid))
    return new_temp, new_salt, new_east, new_north


def cyclic_wraparound_extension(field, width):
    spec = [(width, width), (width, width)] + [(0, 0)] * (field.ndim - 2)
    return jnp.pad(field, spec, mode="wrap")


def reference(potential_thermal_anomaly, saltiness_anomaly, x_boundary_transport_speed, y_boundary_transport_speed, solute_concentrations, ocean_site_indicator, flooded_layer_number):
    levels = jnp.arange(VERTICAL_LAYERS, dtype=jnp.int32)
    wetness = ((ocean_site_indicator[:, :, None] > 0) & (levels[None, None, :] < flooded_layer_number[:, :, None])).astype(jnp.float32)
    flooded_edge_indicator = cyclic_wraparound_extension(wetness, 1)
    for section in range(STEPS):
        thermal_halfway_value, saltiness_anomaly, x_boundary_transport_speed, y_boundary_transport_speed = dynamics_update(
            cyclic_wraparound_extension(potential_thermal_anomaly, 1), cyclic_wraparound_extension(saltiness_anomaly, 1), flooded_edge_indicator, x_boundary_transport_speed, y_boundary_transport_speed)
        tracer_rim = cyclic_wraparound_extension(solute_concentrations, 2)
        east_rim = cyclic_wraparound_extension(x_boundary_transport_speed, 1)
        north_rim = cyclic_wraparound_extension(y_boundary_transport_speed, 1)

        def block(index):
            opening_offset = (index * GROUP_SPAN).astype(jnp.int32)
            piece = lax.dynamic_slice_in_dim(tracer_rim, opening_offset, GROUP_SPAN + 4, 0)
            east_piece = lax.dynamic_slice_in_dim(east_rim, opening_offset, GROUP_SPAN + 2, 0)
            north_piece = lax.dynamic_slice_in_dim(north_rim, opening_offset, GROUP_SPAN + 2, 0)
            thermal_subblock = lax.dynamic_slice_in_dim(thermal_halfway_value, opening_offset, GROUP_SPAN, 0)
            wet_piece = lax.dynamic_slice_in_dim(wetness, opening_offset, GROUP_SPAN, 0)
            return react(advect(piece, east_piece, north_piece), thermal_subblock, wet_piece)

        moved, thermal_energy_sum = lax.map(block, jnp.arange(LONGITUDE_LINES // GROUP_SPAN, dtype=jnp.int32))
        solute_concentrations = moved.reshape(solute_concentrations.shape)
        potential_thermal_anomaly = thermal_halfway_value + thermal_energy_sum.reshape(potential_thermal_anomaly.shape)
    return potential_thermal_anomaly, saltiness_anomaly, x_boundary_transport_speed, y_boundary_transport_speed, solute_concentrations
```

```python
import jax
import jax.numpy as jnp
from jax import lax
from jax.sharding import PartitionSpec as P

STEPS = 2
ADV_STEP = 0.1
DIFFUSION = 0.1
TURN_COS = 0.955336489125606
TURN_SIN = 0.29552020666134
PRESSURE = 0.2
HALINE = 0.8
BIO_STEP = 0.5
WATER_ATT = 0.005
CHLORO_ATT = 0.003
HEATING = 20.0
TEMP_RATE = 0.0633
NUTRIENT_HALF = 0.5
PREY_HALF = 0.5
GRAZING = 0.8
PHYTO_LOSS = 0.1
GRAZER_LOSS = 0.15
ASSIMILATE = 0.3
NTR = 17
ROWS = ("grp", "gy")


def ring_send(block, axis, step):
    names = axis if isinstance(axis, tuple) else (axis,)
    count = 1
    for name in names:
        count *= lax.axis_size(name)
    return lax.ppermute(block, axis, [(i, (i + step) % count) for i in range(count)])


def limiter(first, second):
    return jnp.where(
        first * second > 0, jnp.where(jnp.abs(first) < jnp.abs(second), first, second), 0.0
    )


def face_flux(q, face, axis):
    n = q.shape[axis] - 4

    def cut(a, lo, size):
        return lax.slice_in_dim(a, lo, lo + size, axis=axis)

    diff = cut(q, 1, n + 3) - cut(q, 0, n + 3)
    slope = limiter(cut(diff, 0, n + 2), cut(diff, 1, n + 2))
    left = cut(q, 1, n + 1) + 0.5 * cut(slope, 0, n + 1)
    right = cut(q, 2, n + 1) - 0.5 * cut(slope, 1, n + 1)
    face = face[:, :, None, :]
    flux = jnp.maximum(face, 0.0) * left + jnp.minimum(face, 0.0) * right
    return cut(flux, 1, n) - cut(flux, 0, n)


def react(tracer, temper, wetness):
    depth = tracer.shape[-1]
    upper_rows = lax.broadcasted_iota(jnp.int32, (depth, depth), 0)
    upper_cols = lax.broadcasted_iota(jnp.int32, (depth, depth), 1)
    upper = jnp.where(
        upper_rows < upper_cols, 1.0, jnp.where(upper_rows == upper_cols, 0.5, 0.0)
    ).astype(jnp.float32)
    classes = jnp.arange(8, dtype=jnp.float32)
    theta = (0.3 + 0.1 * classes)[:, None]
    growth_rate = (0.6 + 0.15 * classes)[:, None]
    light_half = (0.1 + 0.1 * classes)[:, None]
    nutrient = tracer[:, :, 0]
    phyto = tracer[:, :, 1:9]
    grazer = tracer[:, :, 9:17]
    chloro = jnp.sum(theta * phyto, axis=2)
    absorb = WATER_ATT + CHLORO_ATT * jnp.abs(chloro)
    optical = jnp.dot(
        absorb, upper, precision=lax.Precision.HIGHEST, preferred_element_type=jnp.float32
    )
    light = jnp.exp(-optical)
    heat = HEATING * absorb * light * wetness
    warm = jnp.exp(TEMP_RATE * temper)
    limit = nutrient / (jnp.abs(nutrient) + NUTRIENT_HALF)
    lit = light[:, :, None]
    growth = growth_rate * (warm * limit)[:, :, None] * lit / (lit + light_half) * phyto
    grazed = GRAZING * grazer * phyto / (jnp.abs(phyto) + PREY_HALF)
    new_phyto = phyto + BIO_STEP * (growth - grazed - PHYTO_LOSS * phyto)
    new_grazer = grazer + BIO_STEP * (ASSIMILATE * grazed - GRAZER_LOSS * grazer)
    new_nutrient = nutrient + BIO_STEP * (
        -jnp.sum(growth, axis=2)
        + PHYTO_LOSS * jnp.sum(phyto, axis=2)
        + GRAZER_LOSS * jnp.sum(grazer, axis=2)
        + (1.0 - ASSIMILATE) * jnp.sum(grazed, axis=2)
    )
    result = (
        jnp.concatenate([new_nutrient[:, :, None], new_phyto, new_grazer], axis=2)
        * wetness[:, :, None]
    )
    return (result, heat)


def to_columns(fields):
    parts = lax.axis_size("gy")
    packed = jnp.stack(fields, axis=2)
    nx, ny, nf, nl = packed.shape
    packed = packed.reshape(nx, parts, ny // parts, nf * nl).transpose(1, 0, 2, 3)
    packed = lax.all_to_all(packed, "gy", split_axis=0, concat_axis=0, tiled=True)
    packed = packed.reshape(parts, nx, ny // parts, nf, nl).transpose(1, 2, 3, 0, 4)
    packed = packed.reshape(nx, ny // parts, nf, parts * nl)
    return [packed[:, :, i] for i in range(nf)]


def to_levels(fields):
    parts = lax.axis_size("gy")
    packed = jnp.stack(fields, axis=2)
    nx, ny, nf, nl = packed.shape
    packed = packed.reshape(nx, ny, nf, parts, nl // parts).transpose(3, 0, 1, 2, 4)
    packed = packed.reshape(parts, nx, ny, nf * nl // parts)
    packed = lax.all_to_all(packed, "gy", split_axis=0, concat_axis=0, tiled=True)
    packed = packed.reshape(parts, nx, ny, nf, nl // parts).transpose(1, 0, 2, 3, 4)
    packed = packed.reshape(nx, parts * ny, nf, nl // parts)
    return tuple(packed[:, :, i] for i in range(nf))


def rims(axis, name, tracer, ahead, behind):
    n = tracer.shape[axis]

    def gather(lines, fields, edge):
        parts = [lax.index_in_dim(tracer, k, axis, keepdims=False) for k in lines]
        parts += [lax.index_in_dim(f, edge, axis, keepdims=False)[:, None] for f in fields]
        return jnp.concatenate(parts, axis=1)

    def open_up(block):
        lines = jnp.stack([block[:, :NTR], block[:, NTR : 2 * NTR]], axis=axis)
        rest = [
            jnp.expand_dims(block[:, k], axis) for k in range(2 * NTR, block.shape[1])
        ]
        return lines, rest

    low = ring_send(gather((n - 2, n - 1), ahead, n - 1), name, 1)
    high = ring_send(gather((0, 1), behind, 0), name, -1)
    return open_up(low), open_up(high)


def on_device(temp, salt, east, north, tracer, mask, bottom):
    levels = tracer.shape[3]
    tile_rows = tracer.shape[1]
    row_start = lax.axis_index("gy") * tile_rows
    mask_tile = lax.dynamic_slice_in_dim(mask, row_start, tile_rows, 1)
    bottom_tile = lax.dynamic_slice_in_dim(bottom, row_start, tile_rows, 1)
    column_levels = lax.broadcasted_iota(jnp.int32, (1, 1, levels), 2)
    wet = ((mask_tile[:, :, None] > 0) & (column_levels < bottom_tile[:, :, None])).astype(
        jnp.float32
    )
    temp, salt, east, north = to_columns([temp, salt, east, north])
    for step in range(STEPS):
        extra = [wet] if step == 0 else []
        ahead = [temp, salt, east, north] + extra
        behind = [temp, salt] + extra
        (t_west, f_west), (t_east, f_east) = rims(0, "gx", tracer, ahead, behind)
        (t_south, f_south), (t_north, f_north) = rims(1, ROWS, tracer, ahead, behind)
        if step == 0:
            wet_x = jnp.concatenate([f_west[4], wet, f_east[2]], axis=0)
            wet_y = jnp.concatenate([f_south[4], wet, f_north[2]], axis=1)
            open_x = wet_x[:-1] * wet_x[1:]
            open_y = wet_y[:, :-1] * wet_y[:, 1:]

        def laplace(q, qx, qy):
            return (
                open_x[1:] * (qx[2:] - q)
                - open_x[:-1] * (q - qx[:-2])
                + open_y[:, 1:] * (qy[:, 2:] - q)
                - open_y[:, :-1] * (q - qy[:, :-2])
            )

        temp_x = jnp.concatenate([f_west[0], temp, f_east[0]], axis=0)
        salt_x = jnp.concatenate([f_west[1], salt, f_east[1]], axis=0)
        temp_y = jnp.concatenate([f_south[0], temp, f_north[0]], axis=1)
        salt_y = jnp.concatenate([f_south[1], salt, f_north[1]], axis=1)
        buoy_x = temp_x - HALINE * salt_x
        buoy_y = temp_y - HALINE * salt_y
        halfway = wet * (temp + DIFFUSION * laplace(temp, temp_x, temp_y))
        salt = wet * (salt + DIFFUSION * laplace(salt, salt_x, salt_y))
        face_x = open_x * (
            TURN_COS * jnp.concatenate([f_west[2], east], axis=0)
            + TURN_SIN * jnp.concatenate([f_west[3], north], axis=0)
            - PRESSURE * (buoy_x[1:] - buoy_x[:-1])
        )
        face_y = open_y * (
            -TURN_SIN * jnp.concatenate([f_south[2], east], axis=1)
            + TURN_COS * jnp.concatenate([f_south[3], north], axis=1)
            - PRESSURE * (buoy_y[:, 1:] - buoy_y[:, :-1])
        )
        east, north = face_x[1:], face_y[:, 1:]
        moved = tracer - ADV_STEP * (
            face_flux(jnp.concatenate([t_west, tracer, t_east], axis=0), face_x, 0)
            + face_flux(jnp.concatenate([t_south, tracer, t_north], axis=1), face_y, 1)
        )
        tracer, heat = react(moved, halfway, wet)
        temp = halfway + heat
    temp, salt, east, north = to_levels([temp, salt, east, north])
    return temp, salt, east, north, tracer


def solution(mesh):
    field = P("gx", "grp", "gy")
    tracers = P("gx", ("grp", "gy"), None, None)
    columns = P("gx", "grp")
    return jax.shard_map(
        on_device,
        mesh=mesh,
        in_specs=(field, field, field, field, tracers, columns, columns),
        out_specs=(field, field, field, field, tracers),
    )
```

```python
import jax
import jax.numpy as jnp
from jax import lax
from jax.sharding import PartitionSpec as P

STEPS = 2
ADV_STEP = 0.1
DIFFUSION = 0.1
TURN_COS = 0.955336489125606
TURN_SIN = 0.29552020666134
PRESSURE = 0.2
HALINE = 0.8
BIO_STEP = 0.5
WATER_ATT = 0.005
CHLORO_ATT = 0.003
HEATING = 20.0
TEMP_RATE = 0.0633
NUTRIENT_HALF = 0.5
PREY_HALF = 0.5
GRAZING = 0.8
PHYTO_LOSS = 0.1
GRAZER_LOSS = 0.15
ASSIMILATE = 0.3
NTR = 17
ROWS = ("grp", "gy")


def ring_send(block, axis, step):
    names = axis if isinstance(axis, tuple) else (axis,)
    count = 1
    for name in names:
        count *= lax.axis_size(name)
    return lax.ppermute(block, axis, [(i, (i + step) % count) for i in range(count)])


def limiter(first, second):
    return jnp.where(
        first * second > 0, jnp.where(jnp.abs(first) < jnp.abs(second), first, second), 0.0
    )


def face_flux(q, face, axis):
    n = q.shape[axis] - 4

    def cut(a, lo, size):
        return lax.slice_in_dim(a, lo, lo + size, axis=axis)

    diff = cut(q, 1, n + 3) - cut(q, 0, n + 3)
    slope = limiter(cut(diff, 0, n + 2), cut(diff, 1, n + 2))
    left = cut(q, 1, n + 1) + 0.5 * cut(slope, 0, n + 1)
    right = cut(q, 2, n + 1) - 0.5 * cut(slope, 1, n + 1)
    face = face[:, :, None, :]
    flux = jnp.maximum(face, 0.0) * left + jnp.minimum(face, 0.0) * right
    return cut(flux, 1, n) - cut(flux, 0, n)


def advect(q, face_x, face_y):
    return q[2:-2, 2:-2] - ADV_STEP * (
        face_flux(q[:, 2:-2], face_x, 0) + face_flux(q[2:-2], face_y, 1)
    )


def dynamics(temp, salt, wet, east, north):
    open_x = wet[:-1] * wet[1:]
    open_y = wet[:, :-1] * wet[:, 1:]
    inner = wet[1:-1, 1:-1]

    def diffuse(q):
        step_x = (open_x * (q[1:] - q[:-1]))[:, 1:-1]
        step_y = (open_y * (q[:, 1:] - q[:, :-1]))[1:-1]
        lap = step_x[1:] - step_x[:-1] + step_y[:, 1:] - step_y[:, :-1]
        return inner * (q[1:-1, 1:-1] + DIFFUSION * lap)

    buoy = temp - HALINE * salt
    face_x = open_x * (
        TURN_COS * east[:-1] + TURN_SIN * north[:-1] - PRESSURE * (buoy[1:] - buoy[:-1])
    )
    face_y = open_y * (
        -TURN_SIN * east[:, :-1] + TURN_COS * north[:, :-1]
        - PRESSURE * (buoy[:, 1:] - buoy[:, :-1])
    )
    return diffuse(temp), diffuse(salt), face_x, face_y


def react(tracer, temper, wetness):
    depth = tracer.shape[-1]
    upper_rows = lax.broadcasted_iota(jnp.int32, (depth, depth), 0)
    upper_cols = lax.broadcasted_iota(jnp.int32, (depth, depth), 1)
    upper = jnp.where(
        upper_rows < upper_cols, 1.0, jnp.where(upper_rows == upper_cols, 0.5, 0.0)
    ).astype(jnp.float32)
    classes = jnp.arange(8, dtype=jnp.float32)
    theta = (0.3 + 0.1 * classes)[:, None]
    growth_rate = (0.6 + 0.15 * classes)[:, None]
    light_half = (0.1 + 0.1 * classes)[:, None]
    nutrient = tracer[:, :, 0]
    phyto = tracer[:, :, 1:9]
    grazer = tracer[:, :, 9:17]
    chloro = jnp.sum(theta * phyto, axis=2)
    absorb = WATER_ATT + CHLORO_ATT * jnp.abs(chloro)
    optical = jnp.dot(
        absorb, upper, precision=lax.Precision.HIGHEST, preferred_element_type=jnp.float32
    )
    light = jnp.exp(-optical)
    heat = HEATING * absorb * light * wetness
    warm = jnp.exp(TEMP_RATE * temper)
    limit = nutrient / (jnp.abs(nutrient) + NUTRIENT_HALF)
    lit = light[:, :, None]
    growth = growth_rate * (warm * limit)[:, :, None] * lit / (lit + light_half) * phyto
    grazed = GRAZING * grazer * phyto / (jnp.abs(phyto) + PREY_HALF)
    new_phyto = phyto + BIO_STEP * (growth - grazed - PHYTO_LOSS * phyto)
    new_grazer = grazer + BIO_STEP * (ASSIMILATE * grazed - GRAZER_LOSS * grazer)
    new_nutrient = nutrient + BIO_STEP * (
        -jnp.sum(growth, axis=2)
        + PHYTO_LOSS * jnp.sum(phyto, axis=2)
        + GRAZER_LOSS * jnp.sum(grazer, axis=2)
        + (1.0 - ASSIMILATE) * jnp.sum(grazed, axis=2)
    )
    result = (
        jnp.concatenate([new_nutrient[:, :, None], new_phyto, new_grazer], axis=2)
        * wetness[:, :, None]
    )
    return (result, heat)


def to_columns(fields):
    parts = lax.axis_size("gy")
    packed = jnp.stack(fields, axis=2)
    nx, ny, nf, nl = packed.shape
    packed = packed.reshape(nx, parts, ny // parts, nf * nl).transpose(1, 0, 2, 3)
    packed = lax.all_to_all(packed, "gy", split_axis=0, concat_axis=0, tiled=True)
    packed = packed.reshape(parts, nx, ny // parts, nf, nl).transpose(1, 2, 3, 0, 4)
    packed = packed.reshape(nx, ny // parts, nf, parts * nl)
    return [packed[:, :, i] for i in range(nf)]


def to_levels(fields):
    parts = lax.axis_size("gy")
    packed = jnp.stack(fields, axis=2)
    nx, ny, nf, nl = packed.shape
    packed = packed.reshape(nx, ny, nf, parts, nl // parts).transpose(3, 0, 1, 2, 4)
    packed = packed.reshape(parts, nx, ny, nf * nl // parts)
    packed = lax.all_to_all(packed, "gy", split_axis=0, concat_axis=0, tiled=True)
    packed = packed.reshape(parts, nx, ny, nf, nl // parts).transpose(1, 0, 2, 3, 4)
    packed = packed.reshape(nx, parts * ny, nf, nl // parts)
    return tuple(packed[:, :, i] for i in range(nf))


def flat(*pieces):
    return jnp.concatenate([p.reshape(-1, p.shape[-1]) for p in pieces], axis=0)


def unflat(block, *shapes):
    out, at = [], 0
    for shape in shapes:
        size = 1
        for length in shape[:-1]:
            size *= length
        out.append(block[at : at + size].reshape(shape))
        at += size
    return out


def on_device(temp, salt, east, north, tracer, mask, bottom):
    nx, ny, ntr, levels = tracer.shape
    row_start = lax.axis_index("gy") * ny
    mask_tile = lax.dynamic_slice_in_dim(mask, row_start, ny, 1)
    bottom_tile = lax.dynamic_slice_in_dim(bottom, row_start, ny, 1)
    column_levels = lax.broadcasted_iota(jnp.int32, (1, 1, levels), 2)
    wet = ((mask_tile[:, :, None] > 0) & (column_levels < bottom_tile[:, :, None])).astype(
        jnp.float32
    )
    west = ring_send(tracer, "gx", 1)
    east_t = ring_send(tracer, "gx", -1)

    temp, salt, east, north = to_columns([temp, salt, east, north])
    state = jnp.stack([temp, salt, wet, east, north], axis=0)

    y_shapes = ((nx, 4, ntr, levels), (5, nx, 3, levels))
    south, s_state = unflat(
        ring_send(flat(tracer[:, ny - 4 :], state[:, :, ny - 3 :]), ROWS, 1), *y_shapes
    )
    north_t, n_state = unflat(
        ring_send(flat(tracer[:, :4], state[:, :, :3]), ROWS, -1), *y_shapes
    )
    state = jnp.concatenate([s_state, state, n_state], axis=2)

    x_shapes = ((2, 2, ntr, levels), (2, 2, ntr, levels), (5, 3, ny + 4, levels))
    sw, nw, w_state = unflat(
        ring_send(
            flat(south[nx - 2 :, 2:], north_t[nx - 2 :, :2], state[:, nx - 3 :, 1:-1]), "gx", 1
        ),
        *x_shapes,
    )
    se, ne, e_state = unflat(
        ring_send(flat(south[:2, 2:], north_t[:2, :2], state[:, :3, 1:-1]), "gx", -1), *x_shapes
    )
    pad = ((0, 0), (0, 0), (1, 1), (0, 0))
    state = jnp.concatenate([jnp.pad(w_state, pad), state, jnp.pad(e_state, pad)], axis=1)
    corner = [
        jnp.pad(sw, ((2, 0), (2, 0), (0, 0), (0, 0))),
        jnp.pad(se, ((0, 2), (2, 0), (0, 0), (0, 0))),
        jnp.pad(nw, ((2, 0), (0, 2), (0, 0), (0, 0))),
        jnp.pad(ne, ((0, 2), (0, 2), (0, 0), (0, 0))),
    ]
    tracer = jnp.concatenate(
        [
            jnp.concatenate([corner[0], south, corner[1]], axis=0),
            jnp.concatenate([west, tracer, east_t], axis=0),
            jnp.concatenate([corner[2], north_t, corner[3]], axis=0),
        ],
        axis=1,
    )
    temp, salt, wet, east, north = [state[i] for i in range(5)]
    for step in range(STEPS):
        halfway, salt, east, north = dynamics(temp, salt, wet, east, north)
        east, north = east[:, 1:-1], north[1:-1]
        wet = wet[1:-1, 1:-1]
        tracer, heat = react(advect(tracer, east, north), halfway, wet)
        temp = halfway + heat
        east, north = east[1:], north[:, 1:]
        if step + 1 < STEPS:
            temp, salt, wet, east, north = [
                f[1:-1, 1:-1] for f in (temp, salt, wet, east, north)
            ]
    temp, salt, east, north = to_levels([temp, salt, east, north])
    return temp, salt, east, north, tracer


def solution(mesh):
    field = P("gx", "grp", "gy")
    tracers = P("gx", ("grp", "gy"), None, None)
    columns = P("gx", "grp")
    return jax.shard_map(
        on_device,
        mesh=mesh,
        in_specs=(field, field, field, field, tracers, columns, columns),
        out_specs=(field, field, field, field, tracers),
    )
```

```python
import jax
import jax.numpy as jnp
from jax import lax
from jax.experimental import pallas as pl
from jax.experimental.pallas import tpu as pltpu
from jax.sharding import PartitionSpec as P

STEPS = 2
ADV_STEP = 0.1
DIFFUSION = 0.1
TURN_COS = 0.955336489125606
TURN_SIN = 0.29552020666134
PRESSURE = 0.2
HALINE = 0.8
BIO_STEP = 0.5
WATER_ATT = 0.005
CHLORO_ATT = 0.003
HEATING = 20.0
TEMP_RATE = 0.0633
NUTRIENT_HALF = 0.5
PREY_HALF = 0.5
GRAZING = 0.8
PHYTO_LOSS = 0.1
GRAZER_LOSS = 0.15
ASSIMILATE = 0.3
NTR = 17
ROWS = ("grp", "gy")


def ring_send(block, axis, step):
    names = axis if isinstance(axis, tuple) else (axis,)
    count = 1
    for name in names:
        count *= lax.axis_size(name)
    return lax.ppermute(block, axis, [(i, (i + step) % count) for i in range(count)])


def minmod(a, b):
    return jnp.maximum(jnp.minimum(a, b), 0.0) + jnp.minimum(jnp.maximum(a, b), 0.0)


def upwind(face, left, right):
    return face * jnp.where(face > 0, left, right)


def physics_rows(get, rows, put_west, put_east, put_south, put_mid):
    def buoy(row, shift):
        return get(0, row, shift) - HALINE * get(1, row, shift)

    def face_x(row, shift):
        gate = get(2, row, shift) * get(2, row, shift + 1)
        turned = TURN_COS * get(3, row, shift) + TURN_SIN * get(4, row, shift)
        return gate * (turned - PRESSURE * (buoy(row, shift + 1) - buoy(row, shift)))

    def face_y(row):
        gate = get(2, row, 0) * get(2, row + 1, 0)
        turned = TURN_COS * get(4, row, 0) - TURN_SIN * get(3, row, 0)
        return gate * (turned - PRESSURE * (buoy(row + 1, 0) - buoy(row, 0)))

    def body(row, carry):
        put_west(row, face_x(row, -1))
        put_east(row, face_x(row, 0))
        put_south(row, face_y(row - 1))
        wet = get(2, row, 0)
        open_e, open_w = wet * get(2, row, 1), wet * get(2, row, -1)
        open_n, open_s = wet * get(2, row + 1, 0), wet * get(2, row - 1, 0)
        fresh = []
        for f in (0, 1):
            q = get(f, row, 0)
            lap = (
                open_e * (get(f, row, 1) - q)
                - open_w * (q - get(f, row, -1))
                + open_n * (get(f, row + 1, 0) - q)
                - open_s * (q - get(f, row - 1, 0))
            )
            fresh.append(wet * (q + DIFFUSION * lap))
        put_mid(row, *fresh)
        return carry

    lax.fori_loop(0, rows, body, 0)
    put_south(rows, face_y(rows - 1))


def advect_all(src, dst, width, rows, west, east, south):
    def body(t, carry):
        def cell(e, shift=0):
            return src[e, t, 2 + shift : 2 + shift + width, :]

        below, here = cell(1), cell(2)
        d_low = here - below
        left_y = below + 0.5 * minmod(below - cell(0), d_low)
        flux_prev = None
        change_x = None
        q_prev = None
        for e in range(2, rows + 3):
            above = cell(e + 1)
            d_high = above - here
            half = 0.5 * minmod(d_low, d_high)
            flux = upwind(south[e - 2, :width, :], left_y, here - half)
            if flux_prev is not None:
                dst[e - 3, t, :width, :] = q_prev - ADV_STEP * (change_x + (flux - flux_prev))
            if e < rows + 2:
                m2, m1, p1, p2 = cell(e, -2), cell(e, -1), cell(e, 1), cell(e, 2)
                d0, d1, d2, d3 = m1 - m2, here - m1, p1 - here, p2 - p1
                h_m, h_0, h_p = 0.5 * minmod(d0, d1), 0.5 * minmod(d1, d2), 0.5 * minmod(d2, d3)
                change_x = upwind(east[e - 2, :width, :], here + h_0, p1 - h_p) - upwind(
                    west[e - 2, :width, :], m1 + h_m, here - h_0
                )
            flux_prev, q_prev = flux, here
            left_y = here + half
            here, d_low = above, d_high
        return carry

    lax.fori_loop(0, NTR, body, 0)


def absorb_rows(cells, width, rows, absorb):
    def body(row, carry):
        chloro = 0.3 * cells[row, 1, :width, :]
        for c in range(1, 8):
            chloro = chloro + (0.3 + 0.1 * c) * cells[row, 1 + c, :width, :]
        absorb[row, :, :] = WATER_ATT + CHLORO_ATT * jnp.abs(chloro)
        return carry

    lax.fori_loop(0, rows, body, 0)


def dim_light(absorb, light, rows, width):
    depth = absorb.shape[-1]
    above = lax.broadcasted_iota(jnp.int32, (depth, depth), 0)
    level = lax.broadcasted_iota(jnp.int32, (depth, depth), 1)
    upper = jnp.where(above < level, 1.0, jnp.where(above == level, 0.5, 0.0))
    optical = jnp.dot(
        absorb[...].reshape(rows * width, depth),
        upper.astype(jnp.float32),
        precision=lax.Precision.HIGHEST,
        preferred_element_type=jnp.float32,
    )
    light[...] = jnp.exp(-optical).reshape(rows, width, depth)


def react_rows(cells, width, rows, absorb, light, halfway, wetness, put_temp):
    def body(row, carry):
        lit = light[row]
        wet = wetness(row)
        mid = halfway(row)
        nutrient = cells[row, 0, :width, :]
        drive = jnp.exp(TEMP_RATE * mid) * (nutrient / (jnp.abs(nutrient) + NUTRIENT_HALF)) * lit
        change = jnp.zeros_like(nutrient)
        for c in range(8):
            p = cells[row, 1 + c, :width, :]
            z = cells[row, 9 + c, :width, :]
            growth = (0.6 + 0.15 * c) * drive / (lit + (0.1 + 0.1 * c)) * p
            grazed = GRAZING * z * p / (jnp.abs(p) + PREY_HALF)
            change = change + (
                PHYTO_LOSS * p + GRAZER_LOSS * z + (1.0 - ASSIMILATE) * grazed - growth
            )
            cells[row, 1 + c, :width, :] = wet * (
                p + BIO_STEP * (growth - grazed - PHYTO_LOSS * p)
            )
            cells[row, 9 + c, :width, :] = wet * (
                z + BIO_STEP * (ASSIMILATE * grazed - GRAZER_LOSS * z)
            )
        cells[row, 0, :width, :] = wet * (nutrient + BIO_STEP * change)
        put_temp(row, mid + HEATING * absorb[row] * lit * wet)
        return carry

    lax.fori_loop(0, rows, body, 0)


def two_steps(
    own, west, east, south_in, north_in, west_in, east_in, state,
    out, mail,
    src, phys, u_west, u_east, v_south, mid, cells, absorb, light,
    u_west2, u_east2, v_south2, mid2, absorb2, light2, fields,
):
    ny, ntr, nx, depth = own.shape
    ry = ny + 4

    def place(y, carry):
        src[y + 4, :, 0:4, :] = west[y]
        src[y + 4, :, 4:8, :] = own[y]
        src[y + 4, :, 8:12, :] = east[y]
        for f in range(5):
            phys[f, y + 3, 4:8, :] = state[f, y]
        return carry

    lax.fori_loop(0, ny, place, 0)

    def place_rows(t, carry):
        for j in range(4):
            at = pl.multiple_of((j * ntr + t) * 4, 4)
            src[j, t, 4:8, :] = south_in[pl.ds(at, 4), :]
            src[ny + 4 + j, t, 4:8, :] = north_in[pl.ds(at, 4), :]
        for k, top in ((0, 2), (1, ny + 4)):
            for j in range(2):
                at = ((k * 2 + j) * ntr + t) * 2
                src[top + j, t, 2:4, :] = west_in[pl.ds(at, 2), :]
                src[top + j, t, 8:10, :] = east_in[pl.ds(at, 2), :]
        return carry

    lax.fori_loop(0, ntr, place_rows, 0)
    rows_y, rows_x = 16 * ntr, 8 * ntr
    for f in range(5):
        for j in range(3):
            at = rows_y + (f * 3 + j) * 4
            phys[f, j, 4:8, :] = south_in[at : at + 4, :]
            phys[f, ny + 3 + j, 4:8, :] = north_in[at : at + 4, :]
        for y in range(ry):
            at = rows_x + (f * ry + y) * 3
            phys[f, y + 1, 1:4, :] = west_in[at : at + 3, :]
            phys[f, y + 1, 8:11, :] = east_in[at : at + 3, :]

    def get(f, row, shift):
        return phys[f, row + 1, 2 + shift : 10 + shift, :]

    def put(ref):
        def store(row, value):
            ref[row] = value

        return store

    def put_mid(row, temp, salt):
        mid[0, row] = temp
        mid[1, row] = salt

    physics_rows(get, ry, put(u_west), put(u_east), put(v_south), put_mid)
    advect_all(src, cells, 8, ry, u_west, u_east, v_south)
    absorb_rows(cells, 8, ry, absorb)
    dim_light(absorb, light, ry, 8)

    def put_temp(row, value):
        mid[0, row] = value

    react_rows(
        cells, 8, ry, absorb, light, lambda row: mid[0, row], lambda row: get(2, row, 0), put_temp
    )

    def get2(f, row, shift):
        cut = slice(2 + shift, 6 + shift)
        if f < 2:
            return mid[f, row + 2, cut, :]
        if f == 2:
            return phys[2, row + 3, 4 + shift : 8 + shift, :]
        if f == 3:
            return u_east[row + 2, cut, :]
        return v_south[row + 3, cut, :]

    def put_mid2(row, temp, salt):
        mid2[row] = temp
        fields[1, pl.ds(row * 4, 4), :] = salt

    def put_east2(row, value):
        u_east2[row] = value
        fields[2, pl.ds(row * 4, 4), :] = value

    physics_rows(get2, ny, put(u_west2), put_east2, put(v_south2), put_mid2)
    advect_all(cells, out, 4, ny, u_west2, u_east2, v_south2)
    absorb_rows(out, 4, ny, absorb2)
    dim_light(absorb2, light2, ny, 4)

    def put_temp2(row, value):
        fields[0, pl.ds(row * 4, 4), :] = value
        fields[3, pl.ds(row * 4, 4), :] = v_south2[row + 1]

    react_rows(
        out, 4, ny, absorb2, light2, lambda row: mid2[row], lambda row: get2(2, row, 0), put_temp2
    )

    group = lax.broadcasted_iota(jnp.int32, (4 * ny, depth), 1) // 32
    for g in range(4):
        packed = None
        for f in range(4):
            turn = ((f - g) * 32) % depth
            part = fields[f]
            if turn:
                part = pltpu.roll(part, turn, 1)
            packed = part if packed is None else jnp.where(group == f, part, packed)
        mail[g] = packed


def run_two_steps(own, west, east, south, north, w_in, e_in, state):
    ny, ntr, nx, depth = own.shape
    ry = ny + 4
    f32 = jnp.float32
    vmem = pltpu.VMEM
    whole = pl.BlockSpec(memory_space=pltpu.VMEM)
    return pl.pallas_call(
        two_steps,
        out_shape=(
            jax.ShapeDtypeStruct((ny, ntr, nx, depth), f32),
            jax.ShapeDtypeStruct((4, ny * nx, depth), f32),
        ),
        in_specs=[whole] * 8,
        out_specs=(whole, whole),
        scratch_shapes=[
            vmem((ny + 8, ntr, 16, depth), f32),
            vmem((5, ny + 6, 16, depth), f32),
            vmem((ry, 8, depth), f32),
            vmem((ry, 8, depth), f32),
            vmem((ry + 1, 8, depth), f32),
            vmem((2, ry, 8, depth), f32),
            vmem((ry, ntr, 8, depth), f32),
            vmem((ry, 8, depth), f32),
            vmem((ry, 8, depth), f32),
            vmem((ny, nx, depth), f32),
            vmem((ny, nx, depth), f32),
            vmem((ny + 1, nx, depth), f32),
            vmem((ny, nx, depth), f32),
            vmem((ny, nx, depth), f32),
            vmem((ny, nx, depth), f32),
            vmem((4, ny * nx, depth), f32),
        ],
        compiler_params=pltpu.CompilerParams(vmem_limit_bytes=40 * 1024 * 1024),
        name="two_steps",
    )(own, west, east, south, north, w_in, e_in, state)


def flat(*pieces):
    return jnp.concatenate([p.reshape(-1, p.shape[-1]) for p in pieces], axis=0)


def on_device(temp, salt, east, north, tracer, mask, bottom):
    nx, ny, ntr, levels = tracer.shape
    parts = lax.axis_size("gy")
    share = levels // parts
    row_start = lax.axis_index("gy") * ny
    mask_tile = lax.dynamic_slice_in_dim(mask, row_start, ny, 1).T
    bottom_tile = lax.dynamic_slice_in_dim(bottom, row_start, ny, 1).T
    column_levels = lax.broadcasted_iota(jnp.int32, (1, 1, levels), 2)
    wet = ((mask_tile[:, :, None] > 0) & (column_levels < bottom_tile[:, :, None])).astype(
        jnp.float32
    )
    tracer = tracer.transpose(1, 2, 0, 3)
    west_t = ring_send(tracer, "gx", 1)
    east_t = ring_send(tracer, "gx", -1)

    packed = jnp.stack([temp, salt, east, north], axis=2)
    packed = packed.reshape(nx, parts, ny, 4 * share).transpose(1, 2, 0, 3)
    packed = lax.all_to_all(packed, "gy", split_axis=0, concat_axis=0, tiled=True)
    packed = packed.reshape(parts, ny, nx, 4, share).transpose(3, 1, 2, 0, 4)
    packed = packed.reshape(4, ny, nx, levels)
    state = jnp.concatenate([packed[:2], wet[None], packed[2:]], axis=0)

    south = ring_send(flat(tracer[ny - 4 :], state[:, ny - 3 :]), ROWS, 1)
    north = ring_send(flat(tracer[:4], state[:, :3]), ROWS, -1)
    west_t, east_t, south, north, state = lax.optimization_barrier(
        (west_t, east_t, south, north, state)
    )
    rows = 4 * ntr * nx
    south_t = south[:rows].reshape(4, ntr, nx, levels)
    north_t = north[:rows].reshape(4, ntr, nx, levels)
    south_p = south[rows:].reshape(5, 3, nx, levels)
    north_p = north[rows:].reshape(5, 3, nx, levels)
    tall = jnp.concatenate([south_p[:, 1:], state, north_p[:, :2]], axis=1)

    def side(lines, cells):
        return flat(south_t[2:, :, lines], north_t[:2, :, lines], tall[:, :, cells])

    w_in = ring_send(side(slice(nx - 2, nx), slice(nx - 3, nx)), "gx", 1)
    e_in = ring_send(side(slice(0, 2), slice(0, 3)), "gx", -1)
    tracer, mail = run_two_steps(tracer, west_t, east_t, south, north, w_in, e_in, state)
    mail = lax.all_to_all(mail, "gy", split_axis=0, concat_axis=0, tiled=True)
    mail = mail.reshape(parts, ny, nx, 4, share).transpose(3, 2, 0, 1, 4)
    mail = mail.reshape(4, nx, parts * ny, share)
    fields = [mail[i] for i in range(4)]
    return (*fields, tracer.transpose(2, 0, 1, 3))


def solution(mesh):
    field = P("gx", "grp", "gy")
    tracers = P("gx", ("grp", "gy"), None, None)
    columns = P("gx", "grp")
    return jax.shard_map(
        on_device,
        mesh=mesh,
        in_specs=(field, field, field, field, tracers, columns, columns),
        out_specs=(field, field, field, field, tracers),
        check_vma=False,
    )
```

```python
import jax
import jax.numpy as jnp
from jax import lax
from jax.experimental import pallas as pl
from jax.experimental.pallas import tpu as pltpu
from jax.sharding import PartitionSpec as P

STEPS = 2
ADV_STEP = 0.1
DIFFUSION = 0.1
TURN_COS = 0.955336489125606
TURN_SIN = 0.29552020666134
PRESSURE = 0.2
HALINE = 0.8
BIO_STEP = 0.5
WATER_ATT = 0.005
CHLORO_ATT = 0.003
HEATING = 20.0
TEMP_RATE = 0.0633
NUTRIENT_HALF = 0.5
PREY_HALF = 0.5
GRAZING = 0.8
PHYTO_LOSS = 0.1
GRAZER_LOSS = 0.15
ASSIMILATE = 0.3
NTR = 17
ROWS = ("grp", "gy")


def ring_send(block, axis, step):
    names = axis if isinstance(axis, tuple) else (axis,)
    count = 1
    for name in names:
        count *= lax.axis_size(name)
    return lax.ppermute(block, axis, [(i, (i + step) % count) for i in range(count)])


def minmod(a, b):
    return jnp.maximum(jnp.minimum(a, b), 0.0) + jnp.minimum(jnp.maximum(a, b), 0.0)


def upwind(face, left, right):
    return face * jnp.where(face > 0, left, right)


def physics_rows(get, rows, put_west, put_east, put_south, put_mid):
    def buoy(row, shift):
        return get(0, row, shift) - HALINE * get(1, row, shift)

    def face_x(row, shift):
        gate = get(2, row, shift) * get(2, row, shift + 1)
        turned = TURN_COS * get(3, row, shift) + TURN_SIN * get(4, row, shift)
        return gate * (turned - PRESSURE * (buoy(row, shift + 1) - buoy(row, shift)))

    def face_y(row):
        gate = get(2, row, 0) * get(2, row + 1, 0)
        turned = TURN_COS * get(4, row, 0) - TURN_SIN * get(3, row, 0)
        return gate * (turned - PRESSURE * (buoy(row + 1, 0) - buoy(row, 0)))

    def body(row, carry):
        put_west(row, face_x(row, -1))
        put_east(row, face_x(row, 0))
        put_south(row, face_y(row - 1))
        wet = get(2, row, 0)
        open_e, open_w = wet * get(2, row, 1), wet * get(2, row, -1)
        open_n, open_s = wet * get(2, row + 1, 0), wet * get(2, row - 1, 0)
        fresh = []
        for f in (0, 1):
            q = get(f, row, 0)
            lap = (
                open_e * (get(f, row, 1) - q)
                - open_w * (q - get(f, row, -1))
                + open_n * (get(f, row + 1, 0) - q)
                - open_s * (q - get(f, row - 1, 0))
            )
            fresh.append(wet * (q + DIFFUSION * lap))
        put_mid(row, *fresh)
        return carry

    lax.fori_loop(0, rows, body, 0)
    put_south(rows, face_y(rows - 1))


def advect_all(src, dst, width, rows, west, east, south):
    def body(t, carry):
        def cell(e, shift=0):
            return src[e, t, 2 + shift : 2 + shift + width, :]

        below, here = cell(1), cell(2)
        d_low = here - below
        left_y = below + 0.5 * minmod(below - cell(0), d_low)
        flux_prev = None
        change_x = None
        q_prev = None
        for e in range(2, rows + 3):
            above = cell(e + 1)
            d_high = above - here
            half = 0.5 * minmod(d_low, d_high)
            flux = upwind(south[e - 2, :width, :], left_y, here - half)
            if flux_prev is not None:
                dst[e - 3, t, :width, :] = q_prev - ADV_STEP * (change_x + (flux - flux_prev))
            if e < rows + 2:
                m2, m1, p1, p2 = cell(e, -2), cell(e, -1), cell(e, 1), cell(e, 2)
                d0, d1, d2, d3 = m1 - m2, here - m1, p1 - here, p2 - p1
                h_m, h_0, h_p = 0.5 * minmod(d0, d1), 0.5 * minmod(d1, d2), 0.5 * minmod(d2, d3)
                change_x = upwind(east[e - 2, :width, :], here + h_0, p1 - h_p) - upwind(
                    west[e - 2, :width, :], m1 + h_m, here - h_0
                )
            flux_prev, q_prev = flux, here
            left_y = here + half
            here, d_low = above, d_high
        return carry

    lax.fori_loop(0, NTR, body, 0)


def absorb_rows(cells, width, rows, absorb):
    def body(row, carry):
        chloro = 0.3 * cells[row, 1, :width, :]
        for c in range(1, 8):
            chloro = chloro + (0.3 + 0.1 * c) * cells[row, 1 + c, :width, :]
        absorb[row, :, :] = WATER_ATT + CHLORO_ATT * jnp.abs(chloro)
        return carry

    lax.fori_loop(0, rows, body, 0)


def dim_light(absorb, light, rows, width):
    depth = absorb.shape[-1]
    above = lax.broadcasted_iota(jnp.int32, (depth, depth), 0)
    level = lax.broadcasted_iota(jnp.int32, (depth, depth), 1)
    upper = jnp.where(above < level, 1.0, jnp.where(above == level, 0.5, 0.0))
    optical = jnp.dot(
        absorb[...].reshape(rows * width, depth),
        upper.astype(jnp.float32),
        precision=lax.Precision.HIGHEST,
        preferred_element_type=jnp.float32,
    )
    light[...] = jnp.exp(-optical).reshape(rows, width, depth)


def react_rows(cells, width, rows, absorb, light, halfway, wetness, put_temp):
    def body(row, carry):
        lit = light[row]
        wet = wetness(row)
        mid = halfway(row)
        nutrient = cells[row, 0, :width, :]
        drive = jnp.exp(TEMP_RATE * mid) * (nutrient / (jnp.abs(nutrient) + NUTRIENT_HALF)) * lit
        change = jnp.zeros_like(nutrient)
        for c in range(8):
            p = cells[row, 1 + c, :width, :]
            z = cells[row, 9 + c, :width, :]
            growth = (0.6 + 0.15 * c) * drive / (lit + (0.1 + 0.1 * c)) * p
            grazed = GRAZING * z * p / (jnp.abs(p) + PREY_HALF)
            change = change + (
                PHYTO_LOSS * p + GRAZER_LOSS * z + (1.0 - ASSIMILATE) * grazed - growth
            )
            cells[row, 1 + c, :width, :] = wet * (
                p + BIO_STEP * (growth - grazed - PHYTO_LOSS * p)
            )
            cells[row, 9 + c, :width, :] = wet * (
                z + BIO_STEP * (ASSIMILATE * grazed - GRAZER_LOSS * z)
            )
        cells[row, 0, :width, :] = wet * (nutrient + BIO_STEP * change)
        put_temp(row, mid + HEATING * absorb[row] * lit * wet)
        return carry

    lax.fori_loop(0, rows, body, 0)


def two_steps(
    own, east, west, south_in, north_in, state,
    out, mail,
    src, phys, u_west, u_east, v_south, mid, cells, absorb, light,
    u_west2, u_east2, v_south2, mid2, absorb2, light2, fields,
):
    ny, ntr, nx, depth = own.shape
    ry = ny + 4

    def place(y, carry):
        src[y + 4, :, 0:4, :] = west[y]
        src[y + 4, :, 4:8, :] = own[y]
        src[y + 4, :, 8:12, :] = east[y]
        for f in range(5):
            phys[f, y + 3, 0:10, :] = state[pl.ds((f * ny + y) * 10, 10), :]
        return carry

    lax.fori_loop(0, ny, place, 0)

    wing = 4 * ntr * nx

    def place_rows(t, carry):
        for j in range(4):
            at = pl.multiple_of((j * ntr + t) * 4, 4)
            src[j, t, 4:8, :] = south_in[pl.ds(at, 4), :]
            src[ny + 4 + j, t, 4:8, :] = north_in[pl.ds(at, 4), :]
        for j in range(2):
            at = wing + (j * ntr + t) * 4
            src[2 + j, t, 2:4, :] = south_in[pl.ds(at, 2), :]
            src[2 + j, t, 8:10, :] = south_in[pl.ds(at + 2, 2), :]
            src[ny + 4 + j, t, 2:4, :] = north_in[pl.ds(at, 2), :]
            src[ny + 4 + j, t, 8:10, :] = north_in[pl.ds(at + 2, 2), :]
        return carry

    lax.fori_loop(0, ntr, place_rows, 0)
    for f in range(5):
        for j in range(3):
            at = wing + wing // 2 + (f * 3 + j) * 10
            phys[f, j, 0:10, :] = south_in[at : at + 10, :]
            phys[f, ny + 3 + j, 0:10, :] = north_in[at : at + 10, :]

    def get(f, row, shift):
        return phys[f, row + 1, 1 + shift : 9 + shift, :]

    def put(ref):
        def store(row, value):
            ref[row] = value

        return store

    def put_mid(row, temp, salt):
        mid[0, row] = temp
        mid[1, row] = salt

    physics_rows(get, ry, put(u_west), put(u_east), put(v_south), put_mid)
    advect_all(src, cells, 8, ry, u_west, u_east, v_south)
    absorb_rows(cells, 8, ry, absorb)
    dim_light(absorb, light, ry, 8)

    def put_temp(row, value):
        mid[0, row] = value

    react_rows(
        cells, 8, ry, absorb, light, lambda row: mid[0, row], lambda row: get(2, row, 0), put_temp
    )

    def get2(f, row, shift):
        cut = slice(2 + shift, 6 + shift)
        if f < 2:
            return mid[f, row + 2, cut, :]
        if f == 2:
            return phys[2, row + 3, 3 + shift : 7 + shift, :]
        if f == 3:
            return u_east[row + 2, cut, :]
        return v_south[row + 3, cut, :]

    def put_mid2(row, temp, salt):
        mid2[row] = temp
        fields[1, pl.ds(row * 4, 4), :] = salt

    def put_east2(row, value):
        u_east2[row] = value
        fields[2, pl.ds(row * 4, 4), :] = value

    physics_rows(get2, ny, put(u_west2), put_east2, put(v_south2), put_mid2)
    advect_all(cells, out, 4, ny, u_west2, u_east2, v_south2)
    absorb_rows(out, 4, ny, absorb2)
    dim_light(absorb2, light2, ny, 4)

    def put_temp2(row, value):
        fields[0, pl.ds(row * 4, 4), :] = value
        fields[3, pl.ds(row * 4, 4), :] = v_south2[row + 1]

    react_rows(
        out, 4, ny, absorb2, light2, lambda row: mid2[row], lambda row: get2(2, row, 0), put_temp2
    )

    group = lax.broadcasted_iota(jnp.int32, (4 * ny, depth), 1) // 32
    for g in range(4):
        packed = None
        for f in range(4):
            turn = ((f - g) * 32) % depth
            part = fields[f]
            if turn:
                part = pltpu.roll(part, turn, 1)
            packed = part if packed is None else jnp.where(group == f, part, packed)
        mail[g] = packed


def run_two_steps(own, west, east, south, north, state):
    ny, ntr, nx, depth = own.shape
    ry = ny + 4
    f32 = jnp.float32
    vmem = pltpu.VMEM
    whole = pl.BlockSpec(memory_space=pltpu.VMEM)
    return pl.pallas_call(
        two_steps,
        out_shape=(
            jax.ShapeDtypeStruct((ny, ntr, nx, depth), f32),
            jax.ShapeDtypeStruct((4, ny * nx, depth), f32),
        ),
        in_specs=[whole] * 6,
        out_specs=(whole, whole),
        scratch_shapes=[
            vmem((ny + 8, ntr, 16, depth), f32),
            vmem((5, ny + 6, 16, depth), f32),
            vmem((ry, 8, depth), f32),
            vmem((ry, 8, depth), f32),
            vmem((ry + 1, 8, depth), f32),
            vmem((2, ry, 8, depth), f32),
            vmem((ry, ntr, 8, depth), f32),
            vmem((ry, 8, depth), f32),
            vmem((ry, 8, depth), f32),
            vmem((ny, nx, depth), f32),
            vmem((ny, nx, depth), f32),
            vmem((ny + 1, nx, depth), f32),
            vmem((ny, nx, depth), f32),
            vmem((ny, nx, depth), f32),
            vmem((ny, nx, depth), f32),
            vmem((4, ny * nx, depth), f32),
        ],
        compiler_params=pltpu.CompilerParams(vmem_limit_bytes=40 * 1024 * 1024),
        name="two_steps",
    )(own, east, west, south, north, state)


def call(body, out_shapes, *args, name):
    whole = pl.BlockSpec(memory_space=pltpu.VMEM)
    return pl.pallas_call(
        body,
        out_shape=tuple(jax.ShapeDtypeStruct(s, jnp.float32) for s in out_shapes),
        in_specs=[whole] * len(args),
        out_specs=(whole,) * len(out_shapes),
        compiler_params=pltpu.CompilerParams(vmem_limit_bytes=16 * 1024 * 1024),
        name=name,
    )(*args)


def pack_levels(stacked, own, to_east, to_west):
    span = stacked.shape[1]
    depth = own.shape[1]
    nx = own.shape[0] // span
    for x in range(nx):
        rows = stacked[x * depth : (x + 1) * depth, :].T
        own[x * span : (x + 1) * span, :] = rows
        if x > 0:
            to_east[(x - 1) * span : x * span, :] = rows
        if x < nx - 1:
            to_west[x * span : (x + 1) * span, :] = rows
    for ref in (to_east, to_west):
        ref[3 * span : 3 * span + nx, :] = jnp.zeros((nx, depth), jnp.float32)
        ref[3 * span : 3 * span + nx, 0:span] = stacked[nx * depth :, :]


def stage_mail(own, west, east, mail):
    ny = own.shape[0] // 4
    for x in range(10):
        ref, at = (west, x) if x < 3 else (own, x - 3) if x < 7 else (east, x - 7)
        mail[pl.ds(x, ny, stride=10), :] = ref[at * ny : (at + 1) * ny, :]


def open_mail(mail, wet, own, east, west, state, up, down):
    ny, ntr, nx, depth = own.shape
    cells = ny * 10
    group = lax.broadcasted_iota(jnp.int32, (cells, depth), 1) // 32
    for f, at in ((0, 0), (1, 1), (2, 3), (3, 4)):
        field = None
        for s in range(4):
            turn = ((s - f) * 32) % depth
            part = mail[s]
            if turn:
                part = pltpu.roll(part, turn, 1)
            field = part if field is None else jnp.where(group == s, part, field)
        state[at * cells : (at + 1) * cells, :] = field
    state[2 * cells : 3 * cells, :] = wet[...]
    for j in range(4):
        for t in range(ntr):
            at = (j * ntr + t) * 4
            up[at : at + 4, :] = own[ny - 4 + j, t]
            down[at : at + 4, :] = own[j, t]
    base = 16 * ntr
    for j in range(2):
        for t in range(ntr):
            at = base + (j * ntr + t) * 4
            up[at : at + 2, :] = west[ny - 2 + j, t, 2:4, :]
            up[at + 2 : at + 4, :] = east[ny - 2 + j, t, 0:2, :]
            down[at : at + 2, :] = west[j, t, 2:4, :]
            down[at + 2 : at + 4, :] = east[j, t, 0:2, :]
    base = 24 * ntr
    for f in range(5):
        up[base + f * 30 : base + f * 30 + 30, :] = state[(f + 1) * cells - 30 : (f + 1) * cells, :]
        down[base + f * 30 : base + f * 30 + 30, :] = state[f * cells : f * cells + 30, :]


def unpack_levels(mail, temp, salt, east, north):
    nx, share, ny = temp.shape
    for x in range(nx):
        tall = mail[pl.ds(x, ny, stride=nx), :].T
        for f, ref in enumerate((temp, salt, east, north)):
            ref[x] = tall[f * share : (f + 1) * share]


def on_device(temp, salt, east, north, tracer, mask, bottom):
    nx, ny, ntr, levels = tracer.shape
    parts = lax.axis_size("gy")
    share = levels // parts
    span = parts * ny
    tracer = tracer.transpose(1, 2, 0, 3)

    deep = jnp.where(mask > 0, bottom, 0).astype(jnp.float32)
    stacked = jnp.stack([f.transpose(0, 2, 1) for f in (temp, salt, east, north)], axis=1)
    stacked = jnp.concatenate([stacked.reshape(nx * levels, span), deep], axis=0)
    side = (3 * span + nx, levels)
    own, to_east, to_west = call(
        pack_levels, [(nx * span, levels), side, side], stacked, name="pack_levels"
    )
    west_p = ring_send(to_east, "gx", 1)
    west_t = ring_send(tracer, "gx", 1)
    east_p = ring_send(to_west, "gx", -1)
    east_t = ring_send(tracer, "gx", -1)
    (mail,) = call(stage_mail, [(10 * span, levels)], own, west_p, east_p, name="stage_mail")
    mail = lax.all_to_all(
        mail.reshape(parts, 10 * ny, levels), "gy", split_axis=0, concat_axis=0, tiled=True
    )
    deep = jnp.concatenate(
        [west_p[3 * span + 1 : 3 * span + 4, :span], deep, east_p[3 * span : 3 * span + 3, :span]]
    )
    deep = lax.dynamic_slice_in_dim(deep, lax.axis_index("gy") * ny, ny, 1).T
    level = lax.broadcasted_iota(jnp.int32, (ny, 10, levels), 2).astype(jnp.float32)
    wet = (level < deep[:, :, None]).astype(jnp.float32).reshape(10 * ny, levels)
    y_rows = 24 * ntr + 150
    state, up, down = call(
        open_mail,
        [(50 * ny, levels), (y_rows, levels), (y_rows, levels)],
        mail,
        wet,
        tracer,
        east_t,
        west_t,
        name="open_mail",
    )
    south = ring_send(up, ROWS, 1)
    north = ring_send(down, ROWS, -1)
    tracer, mail = run_two_steps(tracer, west_t, east_t, south, north, state)
    mail = lax.all_to_all(mail, "gy", split_axis=0, concat_axis=0, tiled=True)
    fields = call(
        unpack_levels,
        [(nx, share, span)] * 4,
        mail.reshape(nx * span, levels),
        name="unpack_levels",
    )
    return (*[f.transpose(0, 2, 1) for f in fields], tracer.transpose(2, 0, 1, 3))


def solution(mesh):
    field = P("gx", "grp", "gy")
    tracers = P("gx", ("grp", "gy"), None, None)
    columns = P("gx", "grp")
    return jax.shard_map(
        on_device,
        mesh=mesh,
        in_specs=(field, field, field, field, tracers, columns, columns),
        out_specs=(field, field, field, field, tracers),
        check_vma=False,
    )
```

```python
import jax
import jax.numpy as jnp
from jax import lax
from jax.experimental import pallas as pl
from jax.experimental.pallas import tpu as pltpu
from jax.sharding import PartitionSpec as P

STEPS = 2
ADV_STEP = 0.1
DIFFUSION = 0.1
TURN_COS = 0.955336489125606
TURN_SIN = 0.29552020666134
PRESSURE = 0.2
HALINE = 0.8
BIO_STEP = 0.5
WATER_ATT = 0.005
CHLORO_ATT = 0.003
HEATING = 20.0
TEMP_RATE = 0.0633
NUTRIENT_HALF = 0.5
PREY_HALF = 0.5
GRAZING = 0.8
PHYTO_LOSS = 0.1
GRAZER_LOSS = 0.15
ASSIMILATE = 0.3
NTR = 17
ROWS = ("grp", "gy")


def ring_send(block, axis, step):
    names = axis if isinstance(axis, tuple) else (axis,)
    count = 1
    for name in names:
        count *= lax.axis_size(name)
    return lax.ppermute(block, axis, [(i, (i + step) % count) for i in range(count)])


def minmod(a, b):
    return jnp.maximum(jnp.minimum(a, b), 0.0) + jnp.minimum(jnp.maximum(a, b), 0.0)


def upwind(face, left, right):
    return face * jnp.where(face > 0, left, right)


def physics_rows(get, rows, put_west, put_east, put_south, put_mid):
    def buoy(row, shift):
        return get(0, row, shift) - HALINE * get(1, row, shift)

    def face_x(row, shift):
        gate = get(2, row, shift) * get(2, row, shift + 1)
        turned = TURN_COS * get(3, row, shift) + TURN_SIN * get(4, row, shift)
        return gate * (turned - PRESSURE * (buoy(row, shift + 1) - buoy(row, shift)))

    def face_y(row):
        gate = get(2, row, 0) * get(2, row + 1, 0)
        turned = TURN_COS * get(4, row, 0) - TURN_SIN * get(3, row, 0)
        return gate * (turned - PRESSURE * (buoy(row + 1, 0) - buoy(row, 0)))

    def body(row, carry):
        put_west(row, face_x(row, -1))
        put_east(row, face_x(row, 0))
        put_south(row, face_y(row - 1))
        wet = get(2, row, 0)
        open_e, open_w = wet * get(2, row, 1), wet * get(2, row, -1)
        open_n, open_s = wet * get(2, row + 1, 0), wet * get(2, row - 1, 0)
        fresh = []
        for f in (0, 1):
            q = get(f, row, 0)
            lap = (
                open_e * (get(f, row, 1) - q)
                - open_w * (q - get(f, row, -1))
                + open_n * (get(f, row + 1, 0) - q)
                - open_s * (q - get(f, row - 1, 0))
            )
            fresh.append(wet * (q + DIFFUSION * lap))
        put_mid(row, *fresh)
        return carry

    lax.fori_loop(0, rows, body, 0)
    put_south(rows, face_y(rows - 1))


def advect_all(read, dst, width, rows, west, east, south):
    def body(t, carry):
        def cell(e, shift=0):
            return read(e, t, 2 + shift)

        below, here = cell(1), cell(2)
        d_low = here - below
        left_y = below + 0.5 * minmod(below - cell(0), d_low)
        flux_prev = None
        change_x = None
        q_prev = None
        for e in range(2, rows + 3):
            above = cell(e + 1)
            d_high = above - here
            half = 0.5 * minmod(d_low, d_high)
            flux = upwind(south[e - 2, :width, :], left_y, here - half)
            if flux_prev is not None:
                dst[e - 3, t, :width, :] = q_prev - ADV_STEP * (change_x + (flux - flux_prev))
            if e < rows + 2:
                m2, m1, p1, p2 = cell(e, -2), cell(e, -1), cell(e, 1), cell(e, 2)
                d0, d1, d2, d3 = m1 - m2, here - m1, p1 - here, p2 - p1
                h_m, h_0, h_p = 0.5 * minmod(d0, d1), 0.5 * minmod(d1, d2), 0.5 * minmod(d2, d3)
                change_x = upwind(east[e - 2, :width, :], here + h_0, p1 - h_p) - upwind(
                    west[e - 2, :width, :], m1 + h_m, here - h_0
                )
            flux_prev, q_prev = flux, here
            left_y = here + half
            here, d_low = above, d_high
        return carry

    lax.fori_loop(0, NTR, body, 0)


def absorb_rows(cells, width, rows, absorb):
    def body(row, carry):
        chloro = 0.3 * cells[row, 1, :width, :]
        for c in range(1, 8):
            chloro = chloro + (0.3 + 0.1 * c) * cells[row, 1 + c, :width, :]
        absorb[row, :, :] = WATER_ATT + CHLORO_ATT * jnp.abs(chloro)
        return carry

    lax.fori_loop(0, rows, body, 0)


def dim_light(absorb, light, rows, width):
    depth = absorb.shape[-1]
    above = lax.broadcasted_iota(jnp.int32, (depth, depth), 0)
    level = lax.broadcasted_iota(jnp.int32, (depth, depth), 1)
    upper = jnp.where(above < level, 1.0, jnp.where(above == level, 0.5, 0.0))
    optical = jnp.dot(
        absorb[...].reshape(rows * width, depth),
        upper.astype(jnp.float32),
        precision=lax.Precision.HIGHEST,
        preferred_element_type=jnp.float32,
    )
    light[...] = jnp.exp(-optical).reshape(rows, width, depth)


def react_rows(cells, width, rows, absorb, light, halfway, wetness, put_temp):
    def body(row, carry):
        lit = light[row]
        wet = wetness(row)
        mid = halfway(row)
        nutrient = cells[row, 0, :width, :]
        drive = jnp.exp(TEMP_RATE * mid) * (nutrient / (jnp.abs(nutrient) + NUTRIENT_HALF)) * lit
        change = jnp.zeros_like(nutrient)
        for c in range(8):
            p = cells[row, 1 + c, :width, :]
            z = cells[row, 9 + c, :width, :]
            growth = (0.6 + 0.15 * c) * drive / (lit + (0.1 + 0.1 * c)) * p
            grazed = GRAZING * z * p / (jnp.abs(p) + PREY_HALF)
            change = change + (
                PHYTO_LOSS * p + GRAZER_LOSS * z + (1.0 - ASSIMILATE) * grazed - growth
            )
            cells[row, 1 + c, :width, :] = wet * (
                p + BIO_STEP * (growth - grazed - PHYTO_LOSS * p)
            )
            cells[row, 9 + c, :width, :] = wet * (
                z + BIO_STEP * (ASSIMILATE * grazed - GRAZER_LOSS * z)
            )
        cells[row, 0, :width, :] = wet * (nutrient + BIO_STEP * change)
        put_temp(row, mid + HEATING * absorb[row] * lit * wet)
        return carry

    lax.fori_loop(0, rows, body, 0)


def store_rows(ref):
    def put(row, value):
        ref[row] = value

    return put


def inner_rows(
    own, east, west, state,
    cells, u_east, v_south, mid,
    src, u_west, absorb, light,
):
    ny, ntr, nx, depth = own.shape
    rows = ny - 4

    def place(y, carry):
        src[y, :, 0:4, :] = west[y]
        src[y, :, 4:8, :] = own[y]
        src[y, :, 8:12, :] = east[y]
        return carry

    lax.fori_loop(0, ny, place, 0)

    def get(f, row, shift):
        return state[pl.ds((f * ny + row + 2) * 10 + 1 + shift, 8), :]

    def put_mid(row, temp, salt):
        mid[0, row] = temp
        mid[1, row] = salt

    def put_temp(row, value):
        mid[0, row] = value

    physics_rows(
        get, rows, store_rows(u_west), store_rows(u_east), store_rows(v_south), put_mid
    )
    advect_all(lambda e, t, x: src[e, t, x : x + 8, :], cells, 8, rows, u_west, u_east, v_south)
    absorb_rows(cells, 8, rows, absorb)
    dim_light(absorb, light, rows, 8)
    react_rows(
        cells, 8, rows, absorb, light, lambda row: mid[0, row], lambda row: get(2, row, 0), put_temp
    )


def outer_rows(
    own, east, west, south_in, north_in, state, cells_in, u_in, v_in, mid_in,
    out, mail,
    src, phys, wets, u_west, u_east, v_south, mid, edge, absorb, light,
    u_west2, u_east2, v_south2, mid2, absorb2, light2, fields,
):
    ny, ntr, nx, depth = own.shape
    inner = ny - 4

    def place(y, carry):
        for k, top, at in ((0, 0, 4), (1, ny - 4, 0)):
            src[k, y + at, :, 0:4, :] = west[top + y]
            src[k, y + at, :, 4:8, :] = own[top + y]
            src[k, y + at, :, 8:12, :] = east[top + y]
        return carry

    lax.fori_loop(0, 4, place, 0)
    wing = 4 * ntr * nx

    def place_rows(t, carry):
        for j in range(4):
            at = pl.multiple_of((j * ntr + t) * 4, 4)
            src[0, j, t, 4:8, :] = south_in[pl.ds(at, 4), :]
            src[1, 4 + j, t, 4:8, :] = north_in[pl.ds(at, 4), :]
        for j in range(2):
            at = wing + (j * ntr + t) * 4
            src[0, 2 + j, t, 2:4, :] = south_in[pl.ds(at, 2), :]
            src[0, 2 + j, t, 8:10, :] = south_in[pl.ds(at + 2, 2), :]
            src[1, 4 + j, t, 2:4, :] = north_in[pl.ds(at, 2), :]
            src[1, 4 + j, t, 8:10, :] = north_in[pl.ds(at + 2, 2), :]
        return carry

    lax.fori_loop(0, ntr, place_rows, 0)
    for f in range(5):
        for j in range(3):
            at = wing + wing // 2 + (f * 3 + j) * 10
            low, high = (f * ny + j) * 10, (f * ny + ny - 3 + j) * 10
            phys[0, f, j, 0:10, :] = south_in[at : at + 10, :]
            phys[0, f, 3 + j, 0:10, :] = state[low : low + 10, :]
            phys[1, f, j, 0:10, :] = state[high : high + 10, :]
            phys[1, f, 3 + j, 0:10, :] = north_in[at : at + 10, :]
    wets[0] = phys[0, 2, 2]
    wets[ny + 1] = phys[1, 2, 3]
    for y in range(ny):
        at = (2 * ny + y) * 10
        wets[y + 1, 0:10, :] = state[at : at + 10, :]
    for y in range(inner):
        mid[0, 4 + y] = mid_in[0, y]
        mid[1, 4 + y] = mid_in[1, y]
        u_east[4 + y] = u_in[y]
        v_south[4 + y] = v_in[y]

    for k, at in ((0, 0), (1, inner + 4)):

        def get(f, row, shift):
            return phys[k, f, row + 1, 1 + shift : 9 + shift, :]

        def put_mid(row, temp, salt):
            mid[0, at + row] = temp
            mid[1, at + row] = salt

        here = pl.ds(at, 4)
        faces = v_south.at[pl.ds(at, 5)]
        physics_rows(
            get,
            4,
            store_rows(u_west.at[pl.ds(4 * k, 4)]),
            store_rows(u_east.at[here]),
            store_rows(faces),
            put_mid,
        )
        advect_all(
            lambda e, t, x: src[k, e, t, x : x + 8, :],
            edge.at[k],
            8,
            4,
            u_west.at[pl.ds(4 * k, 4)],
            u_east.at[here],
            faces,
        )
        absorb_rows(edge.at[k], 8, 4, absorb.at[pl.ds(4 * k, 4)])
    dim_light(absorb, light, 8, 8)
    for k, at in ((0, 0), (1, inner + 4)):

        def put_temp(row, value):
            mid[0, at + row] = value

        react_rows(
            edge.at[k],
            8,
            4,
            absorb.at[pl.ds(4 * k, 4)],
            light.at[pl.ds(4 * k, 4)],
            lambda row: mid[0, at + row],
            lambda row: phys[k, 2, row + 1, 1:9, :],
            put_temp,
        )

    def get2(f, row, shift):
        cut = slice(2 + shift, 6 + shift)
        if f < 2:
            return mid[f, row + 2, cut, :]
        if f == 2:
            return wets[row + 1, 3 + shift : 7 + shift, :]
        if f == 3:
            return u_east[row + 2, cut, :]
        return v_south[row + 3, cut, :]

    def read2(e, t, x):
        if e < 4:
            return edge[0, e, t, x : x + 4, :]
        if e < inner + 4:
            return cells_in[e - 4, t, x : x + 4, :]
        return edge[1, e - inner - 4, t, x : x + 4, :]

    def put_mid2(row, temp, salt):
        mid2[row] = temp
        fields[1, pl.ds(row * 4, 4), :] = salt

    def put_east2(row, value):
        u_east2[row] = value
        fields[2, pl.ds(row * 4, 4), :] = value

    physics_rows(get2, ny, store_rows(u_west2), put_east2, store_rows(v_south2), put_mid2)
    advect_all(read2, out, 4, ny, u_west2, u_east2, v_south2)
    absorb_rows(out, 4, ny, absorb2)
    dim_light(absorb2, light2, ny, 4)

    def put_temp2(row, value):
        fields[0, pl.ds(row * 4, 4), :] = value
        fields[3, pl.ds(row * 4, 4), :] = v_south2[row + 1]

    react_rows(
        out, 4, ny, absorb2, light2, lambda row: mid2[row], lambda row: get2(2, row, 0), put_temp2
    )

    group = lax.broadcasted_iota(jnp.int32, (4 * ny, depth), 1) // 32
    for g in range(4):
        packed = None
        for f in range(4):
            turn = ((f - g) * 32) % depth
            part = fields[f]
            if turn:
                part = pltpu.roll(part, turn, 1)
            packed = part if packed is None else jnp.where(group == f, part, packed)
        mail[g] = packed


def run_inner(own, east, west, state):
    ny, ntr, nx, depth = own.shape
    rows = ny - 4
    return call(
        inner_rows,
        [(rows, ntr, 8, depth), (rows, 8, depth), (rows + 1, 8, depth), (2, rows, 8, depth)],
        own,
        east,
        west,
        state,
        name="inner_rows",
        scratch=[
            (ny, ntr, 16, depth),
            (rows, 8, depth),
            (rows, 8, depth),
            (rows, 8, depth),
        ],
    )


def run_outer(own, east, west, south, north, state, *inner):
    ny, ntr, nx, depth = own.shape
    ry = ny + 4
    return call(
        outer_rows,
        [(ny, ntr, nx, depth), (4, ny * nx, depth)],
        own,
        east,
        west,
        south,
        north,
        state,
        *inner,
        name="outer_rows",
        scratch=[
            (2, 8, ntr, 16, depth),
            (2, 5, 6, 16, depth),
            (ny + 2, 16, depth),
            (8, 8, depth),
            (ry, 8, depth),
            (ry + 1, 8, depth),
            (2, ry, 8, depth),
            (2, 4, ntr, 8, depth),
            (8, 8, depth),
            (8, 8, depth),
            (ny, nx, depth),
            (ny, nx, depth),
            (ny + 1, nx, depth),
            (ny, nx, depth),
            (ny, nx, depth),
            (ny, nx, depth),
            (4, ny * nx, depth),
        ],
    )


def call(body, out_shapes, *args, name, scratch=()):
    whole = pl.BlockSpec(memory_space=pltpu.VMEM)
    return pl.pallas_call(
        body,
        out_shape=tuple(jax.ShapeDtypeStruct(s, jnp.float32) for s in out_shapes),
        in_specs=[whole] * len(args),
        out_specs=(whole,) * len(out_shapes),
        scratch_shapes=[pltpu.VMEM(shape, jnp.float32) for shape in scratch],
        compiler_params=pltpu.CompilerParams(vmem_limit_bytes=40 * 1024 * 1024),
        name=name,
    )(*args)


def pack_levels(stacked, own, to_east, to_west):
    span = stacked.shape[1]
    depth = own.shape[1]
    nx = own.shape[0] // span
    for x in range(nx):
        rows = stacked[x * depth : (x + 1) * depth, :].T
        own[x * span : (x + 1) * span, :] = rows
        if x > 0:
            to_east[(x - 1) * span : x * span, :] = rows
        if x < nx - 1:
            to_west[x * span : (x + 1) * span, :] = rows
    for ref in (to_east, to_west):
        ref[3 * span : 3 * span + nx, :] = jnp.zeros((nx, depth), jnp.float32)
        ref[3 * span : 3 * span + nx, 0:span] = stacked[nx * depth :, :]


def stage_mail(own, west, east, mail):
    ny = own.shape[0] // 4
    for x in range(10):
        ref, at = (west, x) if x < 3 else (own, x - 3) if x < 7 else (east, x - 7)
        mail[pl.ds(x, ny, stride=10), :] = ref[at * ny : (at + 1) * ny, :]


def open_mail(mail, wet, own, east, west, state, up, down):
    ny, ntr, nx, depth = own.shape
    cells = ny * 10
    group = lax.broadcasted_iota(jnp.int32, (cells, depth), 1) // 32
    for f, at in ((0, 0), (1, 1), (2, 3), (3, 4)):
        field = None
        for s in range(4):
            turn = ((s - f) * 32) % depth
            part = mail[s]
            if turn:
                part = pltpu.roll(part, turn, 1)
            field = part if field is None else jnp.where(group == s, part, field)
        state[at * cells : (at + 1) * cells, :] = field
    state[2 * cells : 3 * cells, :] = wet[...]
    for j in range(4):
        for t in range(ntr):
            at = (j * ntr + t) * 4
            up[at : at + 4, :] = own[ny - 4 + j, t]
            down[at : at + 4, :] = own[j, t]
    base = 16 * ntr
    for j in range(2):
        for t in range(ntr):
            at = base + (j * ntr + t) * 4
            up[at : at + 2, :] = west[ny - 2 + j, t, 2:4, :]
            up[at + 2 : at + 4, :] = east[ny - 2 + j, t, 0:2, :]
            down[at : at + 2, :] = west[j, t, 2:4, :]
            down[at + 2 : at + 4, :] = east[j, t, 0:2, :]
    base = 24 * ntr
    for f in range(5):
        up[base + f * 30 : base + f * 30 + 30, :] = state[(f + 1) * cells - 30 : (f + 1) * cells, :]
        down[base + f * 30 : base + f * 30 + 30, :] = state[f * cells : f * cells + 30, :]


def unpack_levels(mail, temp, salt, east, north):
    nx, share, ny = temp.shape
    for x in range(nx):
        tall = mail[pl.ds(x, ny, stride=nx), :].T
        for f, ref in enumerate((temp, salt, east, north)):
            ref[x] = tall[f * share : (f + 1) * share]


def on_device(temp, salt, east, north, tracer, mask, bottom):
    nx, ny, ntr, levels = tracer.shape
    parts = lax.axis_size("gy")
    share = levels // parts
    span = parts * ny
    tracer = tracer.transpose(1, 2, 0, 3)

    deep = jnp.where(mask > 0, bottom, 0).astype(jnp.float32)
    stacked = jnp.stack([f.transpose(0, 2, 1) for f in (temp, salt, east, north)], axis=1)
    stacked = jnp.concatenate([stacked.reshape(nx * levels, span), deep], axis=0)
    side = (3 * span + nx, levels)
    own, to_east, to_west = call(
        pack_levels, [(nx * span, levels), side, side], stacked, name="pack_levels"
    )
    west_p = ring_send(to_east, "gx", 1)
    west_t = ring_send(tracer, "gx", 1)
    east_p = ring_send(to_west, "gx", -1)
    east_t = ring_send(tracer, "gx", -1)
    (mail,) = call(stage_mail, [(10 * span, levels)], own, west_p, east_p, name="stage_mail")
    mail = lax.all_to_all(
        mail.reshape(parts, 10 * ny, levels), "gy", split_axis=0, concat_axis=0, tiled=True
    )
    deep = jnp.concatenate(
        [west_p[3 * span + 1 : 3 * span + 4, :span], deep, east_p[3 * span : 3 * span + 3, :span]]
    )
    deep = lax.dynamic_slice_in_dim(deep, lax.axis_index("gy") * ny, ny, 1).T
    level = lax.broadcasted_iota(jnp.int32, (ny, 10, levels), 2).astype(jnp.float32)
    wet = (level < deep[:, :, None]).astype(jnp.float32).reshape(10 * ny, levels)
    y_rows = 24 * ntr + 150
    state, up, down = call(
        open_mail,
        [(50 * ny, levels), (y_rows, levels), (y_rows, levels)],
        mail,
        wet,
        tracer,
        east_t,
        west_t,
        name="open_mail",
    )
    south = ring_send(up, ROWS, 1)
    north = ring_send(down, ROWS, -1)
    inner = run_inner(tracer, east_t, west_t, state)
    tracer, mail = run_outer(tracer, east_t, west_t, south, north, state, *inner)
    mail = lax.all_to_all(mail, "gy", split_axis=0, concat_axis=0, tiled=True)
    fields = call(
        unpack_levels,
        [(nx, share, span)] * 4,
        mail.reshape(nx * span, levels),
        name="unpack_levels",
    )
    return (*[f.transpose(0, 2, 1) for f in fields], tracer.transpose(2, 0, 1, 3))


def solution(mesh):
    field = P("gx", "grp", "gy")
    tracers = P("gx", ("grp", "gy"), None, None)
    columns = P("gx", "grp")
    return jax.shard_map(
        on_device,
        mesh=mesh,
        in_specs=(field, field, field, field, tracers, columns, columns),
        out_specs=(field, field, field, field, tracers),
        check_vma=False,
    )
```

```python
import jax
import jax.numpy as jnp
from jax import lax
from jax.experimental import pallas as pl
from jax.experimental.pallas import tpu as pltpu
from jax.sharding import PartitionSpec as P

STEPS = 2
ADV_STEP = 0.1
DIFFUSION = 0.1
TURN_COS = 0.955336489125606
TURN_SIN = 0.29552020666134
PRESSURE = 0.2
HALINE = 0.8
BIO_STEP = 0.5
WATER_ATT = 0.005
CHLORO_ATT = 0.003
HEATING = 20.0
TEMP_RATE = 0.0633
NUTRIENT_HALF = 0.5
PREY_HALF = 0.5
GRAZING = 0.8
PHYTO_LOSS = 0.1
GRAZER_LOSS = 0.15
ASSIMILATE = 0.3
NTR = 17
ROWS = ("grp", "gy")


def ring_send(block, axis, step):
    names = axis if isinstance(axis, tuple) else (axis,)
    count = 1
    for name in names:
        count *= lax.axis_size(name)
    return lax.ppermute(block, axis, [(i, (i + step) % count) for i in range(count)])


def minmod(a, b):
    return jnp.maximum(jnp.minimum(a, b), 0.0) + jnp.minimum(jnp.maximum(a, b), 0.0)


def upwind(face, left, right):
    return face * jnp.where(face > 0, left, right)


def physics_rows(get, rows, put_west, put_east, put_south, put_mid):
    def buoy(row, shift):
        return get(0, row, shift) - HALINE * get(1, row, shift)

    def face_x(row, shift):
        gate = get(2, row, shift) * get(2, row, shift + 1)
        turned = TURN_COS * get(3, row, shift) + TURN_SIN * get(4, row, shift)
        return gate * (turned - PRESSURE * (buoy(row, shift + 1) - buoy(row, shift)))

    def face_y(row):
        gate = get(2, row, 0) * get(2, row + 1, 0)
        turned = TURN_COS * get(4, row, 0) - TURN_SIN * get(3, row, 0)
        return gate * (turned - PRESSURE * (buoy(row + 1, 0) - buoy(row, 0)))

    def body(row, carry):
        put_west(row, face_x(row, -1))
        put_east(row, face_x(row, 0))
        put_south(row, face_y(row - 1))
        wet = get(2, row, 0)
        open_e, open_w = wet * get(2, row, 1), wet * get(2, row, -1)
        open_n, open_s = wet * get(2, row + 1, 0), wet * get(2, row - 1, 0)
        fresh = []
        for f in (0, 1):
            q = get(f, row, 0)
            lap = (
                open_e * (get(f, row, 1) - q)
                - open_w * (q - get(f, row, -1))
                + open_n * (get(f, row + 1, 0) - q)
                - open_s * (q - get(f, row - 1, 0))
            )
            fresh.append(wet * (q + DIFFUSION * lap))
        put_mid(row, *fresh)
        return carry

    lax.fori_loop(0, rows, body, 0)
    put_south(rows, face_y(rows - 1))


def advect_all(read, dst, width, rows, west, east, south):
    def body(t, carry):
        def cell(e, shift=0):
            return read(e, t, 2 + shift)

        below, here = cell(1), cell(2)
        d_low = here - below
        left_y = below + 0.5 * minmod(below - cell(0), d_low)
        flux_prev = None
        change_x = None
        q_prev = None
        for e in range(2, rows + 3):
            above = cell(e + 1)
            d_high = above - here
            half = 0.5 * minmod(d_low, d_high)
            flux = upwind(south[e - 2, :width, :], left_y, here - half)
            if flux_prev is not None:
                dst[e - 3, t, :width, :] = q_prev - ADV_STEP * (change_x + (flux - flux_prev))
            if e < rows + 2:
                m2, m1, p1, p2 = cell(e, -2), cell(e, -1), cell(e, 1), cell(e, 2)
                d0, d1, d2, d3 = m1 - m2, here - m1, p1 - here, p2 - p1
                h_m, h_0, h_p = 0.5 * minmod(d0, d1), 0.5 * minmod(d1, d2), 0.5 * minmod(d2, d3)
                change_x = upwind(east[e - 2, :width, :], here + h_0, p1 - h_p) - upwind(
                    west[e - 2, :width, :], m1 + h_m, here - h_0
                )
            flux_prev, q_prev = flux, here
            left_y = here + half
            here, d_low = above, d_high
        return carry

    lax.fori_loop(0, NTR, body, 0)


def absorb_rows(cells, width, rows, absorb):
    def body(row, carry):
        chloro = 0.3 * cells[row, 1, :width, :]
        for c in range(1, 8):
            chloro = chloro + (0.3 + 0.1 * c) * cells[row, 1 + c, :width, :]
        absorb[row, :, :] = WATER_ATT + CHLORO_ATT * jnp.abs(chloro)
        return carry

    lax.fori_loop(0, rows, body, 0)


def dim_light(absorb, light, rows, width):
    depth = absorb.shape[-1]
    above = lax.broadcasted_iota(jnp.int32, (depth, depth), 0)
    level = lax.broadcasted_iota(jnp.int32, (depth, depth), 1)
    upper = jnp.where(above < level, 1.0, jnp.where(above == level, 0.5, 0.0))
    optical = jnp.dot(
        absorb[...].reshape(rows * width, depth),
        upper.astype(jnp.float32),
        precision=lax.Precision.HIGHEST,
        preferred_element_type=jnp.float32,
    )
    light[...] = jnp.exp(-optical).reshape(rows, width, depth)


def react_rows(cells, width, rows, absorb, light, halfway, wetness, put_temp):
    def body(row, carry):
        lit = light[row]
        wet = wetness(row)
        mid = halfway(row)
        nutrient = cells[row, 0, :width, :]
        drive = jnp.exp(TEMP_RATE * mid) * (nutrient / (jnp.abs(nutrient) + NUTRIENT_HALF)) * lit
        change = jnp.zeros_like(nutrient)
        for c in range(8):
            p = cells[row, 1 + c, :width, :]
            z = cells[row, 9 + c, :width, :]
            growth = (0.6 + 0.15 * c) * drive / (lit + (0.1 + 0.1 * c)) * p
            grazed = GRAZING * z * p / (jnp.abs(p) + PREY_HALF)
            change = change + (
                PHYTO_LOSS * p + GRAZER_LOSS * z + (1.0 - ASSIMILATE) * grazed - growth
            )
            cells[row, 1 + c, :width, :] = wet * (
                p + BIO_STEP * (growth - grazed - PHYTO_LOSS * p)
            )
            cells[row, 9 + c, :width, :] = wet * (
                z + BIO_STEP * (ASSIMILATE * grazed - GRAZER_LOSS * z)
            )
        cells[row, 0, :width, :] = wet * (nutrient + BIO_STEP * change)
        put_temp(row, mid + HEATING * absorb[row] * lit * wet)
        return carry

    lax.fori_loop(0, rows, body, 0)


def store_rows(ref):
    def put(row, value):
        ref[row] = value

    return put


def inner_rows(
    own, east, west, state,
    cells, u_east, v_south, mid,
    src, u_west, absorb, light,
):
    ny, ntr, nx, depth = own.shape
    rows = ny - 4

    def place(y, carry):
        src[y, :, 0:4, :] = west[y]
        src[y, :, 4:8, :] = own[y]
        src[y, :, 8:12, :] = east[y]
        return carry

    lax.fori_loop(0, ny, place, 0)

    def get(f, row, shift):
        return state[pl.ds((f * ny + row + 2) * 10 + 1 + shift, 8), :]

    def put_mid(row, temp, salt):
        mid[0, row] = temp
        mid[1, row] = salt

    def put_temp(row, value):
        mid[0, row] = value

    physics_rows(
        get, rows, store_rows(u_west), store_rows(u_east), store_rows(v_south), put_mid
    )
    advect_all(lambda e, t, x: src[e, t, x : x + 8, :], cells, 8, rows, u_west, u_east, v_south)
    absorb_rows(cells, 8, rows, absorb)
    dim_light(absorb, light, rows, 8)
    react_rows(
        cells, 8, rows, absorb, light, lambda row: mid[0, row], lambda row: get(2, row, 0), put_temp
    )


def outer_rows(
    own, east, west, south_in, north_in, state, cells_in, u_in, v_in, mid_in,
    out, mail,
    src, phys, wets, u_west, u_east, v_south, mid, edge, absorb, light,
    u_west2, u_east2, v_south2, mid2, absorb2, light2, fields,
):
    ny, ntr, nx, depth = own.shape
    inner = ny - 4

    def place(y, carry):
        for k, top, at in ((0, 0, 4), (1, ny - 4, 0)):
            src[k, y + at, :, 0:4, :] = west[top + y]
            src[k, y + at, :, 4:8, :] = own[top + y]
            src[k, y + at, :, 8:12, :] = east[top + y]
        return carry

    lax.fori_loop(0, 4, place, 0)
    wing = 4 * ntr * nx

    def place_rows(t, carry):
        for j in range(4):
            at = pl.multiple_of((j * ntr + t) * 4, 4)
            src[0, j, t, 4:8, :] = south_in[pl.ds(at, 4), :]
            src[1, 4 + j, t, 4:8, :] = north_in[pl.ds(at, 4), :]
        for j in range(2):
            at = wing + (j * ntr + t) * 4
            src[0, 2 + j, t, 2:4, :] = south_in[pl.ds(at, 2), :]
            src[0, 2 + j, t, 8:10, :] = south_in[pl.ds(at + 2, 2), :]
            src[1, 4 + j, t, 2:4, :] = north_in[pl.ds(at, 2), :]
            src[1, 4 + j, t, 8:10, :] = north_in[pl.ds(at + 2, 2), :]
        return carry

    lax.fori_loop(0, ntr, place_rows, 0)
    for f in range(5):
        for j in range(3):
            at = wing + wing // 2 + (f * 3 + j) * 10
            low, high = (f * ny + j) * 10, (f * ny + ny - 3 + j) * 10
            phys[0, f, j, 0:10, :] = south_in[at : at + 10, :]
            phys[0, f, 3 + j, 0:10, :] = state[low : low + 10, :]
            phys[1, f, j, 0:10, :] = state[high : high + 10, :]
            phys[1, f, 3 + j, 0:10, :] = north_in[at : at + 10, :]
    wets[0] = phys[0, 2, 2]
    wets[ny + 1] = phys[1, 2, 3]
    for y in range(ny):
        at = (2 * ny + y) * 10
        wets[y + 1, 0:10, :] = state[at : at + 10, :]
    for y in range(inner):
        mid[0, 4 + y] = mid_in[0, y]
        mid[1, 4 + y] = mid_in[1, y]
        u_east[4 + y] = u_in[y]
        v_south[4 + y] = v_in[y]

    for k, at in ((0, 0), (1, inner + 4)):

        def get(f, row, shift):
            return phys[k, f, row + 1, 1 + shift : 9 + shift, :]

        def put_mid(row, temp, salt):
            mid[0, at + row] = temp
            mid[1, at + row] = salt

        here = pl.ds(at, 4)
        faces = v_south.at[pl.ds(at, 5)]
        physics_rows(
            get,
            4,
            store_rows(u_west.at[pl.ds(4 * k, 4)]),
            store_rows(u_east.at[here]),
            store_rows(faces),
            put_mid,
        )
        advect_all(
            lambda e, t, x: src[k, e, t, x : x + 8, :],
            edge.at[k],
            8,
            4,
            u_west.at[pl.ds(4 * k, 4)],
            u_east.at[here],
            faces,
        )
        absorb_rows(edge.at[k], 8, 4, absorb.at[pl.ds(4 * k, 4)])
    dim_light(absorb, light, 8, 8)
    for k, at in ((0, 0), (1, inner + 4)):

        def put_temp(row, value):
            mid[0, at + row] = value

        react_rows(
            edge.at[k],
            8,
            4,
            absorb.at[pl.ds(4 * k, 4)],
            light.at[pl.ds(4 * k, 4)],
            lambda row: mid[0, at + row],
            lambda row: phys[k, 2, row + 1, 1:9, :],
            put_temp,
        )

    def get2(f, row, shift):
        cut = slice(2 + shift, 6 + shift)
        if f < 2:
            return mid[f, row + 2, cut, :]
        if f == 2:
            return wets[row + 1, 3 + shift : 7 + shift, :]
        if f == 3:
            return u_east[row + 2, cut, :]
        return v_south[row + 3, cut, :]

    def read2(e, t, x):
        if e < 4:
            return edge[0, e, t, x : x + 4, :]
        if e < inner + 4:
            return cells_in[e - 4, t, x : x + 4, :]
        return edge[1, e - inner - 4, t, x : x + 4, :]

    def put_mid2(row, temp, salt):
        mid2[row] = temp
        fields[1, pl.ds(row * 4, 4), :] = salt

    def put_east2(row, value):
        u_east2[row] = value
        fields[2, pl.ds(row * 4, 4), :] = value

    physics_rows(get2, ny, store_rows(u_west2), put_east2, store_rows(v_south2), put_mid2)
    advect_all(read2, out, 4, ny, u_west2, u_east2, v_south2)
    absorb_rows(out, 4, ny, absorb2)
    dim_light(absorb2, light2, ny, 4)

    def put_temp2(row, value):
        fields[0, pl.ds(row * 4, 4), :] = value
        fields[3, pl.ds(row * 4, 4), :] = v_south2[row + 1]

    react_rows(
        out, 4, ny, absorb2, light2, lambda row: mid2[row], lambda row: get2(2, row, 0), put_temp2
    )

    group = lax.broadcasted_iota(jnp.int32, (4 * ny, depth), 1) // 32
    for g in range(4):
        packed = None
        for f in range(4):
            turn = ((f - g) * 32) % depth
            part = fields[f]
            if turn:
                part = pltpu.roll(part, turn, 1)
            packed = part if packed is None else jnp.where(group == f, part, packed)
        mail[g] = packed


def run_inner(own, east, west, state):
    ny, ntr, nx, depth = own.shape
    rows = ny - 4
    return call(
        inner_rows,
        [(rows, ntr, 8, depth), (rows, 8, depth), (rows + 1, 8, depth), (2, rows, 8, depth)],
        own,
        east,
        west,
        state,
        name="inner_rows",
        scratch=[
            (ny, ntr, 16, depth),
            (rows, 8, depth),
            (rows, 8, depth),
            (rows, 8, depth),
        ],
    )


def run_outer(own, east, west, south, north, state, *inner):
    ny, ntr, nx, depth = own.shape
    ry = ny + 4
    return call(
        outer_rows,
        [(ny, ntr, nx, depth), (4, ny * nx, depth)],
        own,
        east,
        west,
        south,
        north,
        state,
        *inner,
        name="outer_rows",
        scratch=[
            (2, 8, ntr, 16, depth),
            (2, 5, 6, 16, depth),
            (ny + 2, 16, depth),
            (8, 8, depth),
            (ry, 8, depth),
            (ry + 1, 8, depth),
            (2, ry, 8, depth),
            (2, 4, ntr, 8, depth),
            (8, 8, depth),
            (8, 8, depth),
            (ny, nx, depth),
            (ny, nx, depth),
            (ny + 1, nx, depth),
            (ny, nx, depth),
            (ny, nx, depth),
            (ny, nx, depth),
            (4, ny * nx, depth),
        ],
    )


def call(body, out_shapes, *args, name, scratch=()):
    whole = pl.BlockSpec(memory_space=pltpu.VMEM)
    return pl.pallas_call(
        body,
        out_shape=tuple(jax.ShapeDtypeStruct(s, jnp.float32) for s in out_shapes),
        in_specs=[whole] * len(args),
        out_specs=(whole,) * len(out_shapes),
        scratch_shapes=[pltpu.VMEM(shape, jnp.float32) for shape in scratch],
        compiler_params=pltpu.CompilerParams(vmem_limit_bytes=40 * 1024 * 1024),
        name=name,
    )(*args)


def pack_levels(stacked, tracer, own, to_east, to_west):
    span = stacked.shape[1]
    depth = own.shape[1]
    nx = own.shape[0] // span
    for x in range(nx):
        rows = stacked[x * depth : (x + 1) * depth, :].T
        own[x * span : (x + 1) * span, :] = rows
        if x > 0:
            to_east[(x - 1) * span : x * span, :] = rows
        if x < nx - 1:
            to_west[x * span : (x + 1) * span, :] = rows
    for ref in (to_east, to_west):
        ref[3 * span : 3 * span + nx, :] = jnp.zeros((nx, depth), jnp.float32)
        ref[3 * span : 3 * span + nx, 0:span] = stacked[nx * depth :, :]
    ny, ntr = tracer.shape[:2]
    base = 3 * span + nx
    for k, line in enumerate((0, 1, ny - 2, ny - 1)):
        for t in range(ntr):
            at = base + (k * ntr + t) * 2
            to_east[at : at + 2, :] = tracer[line, t, nx - 2 :, :]
            to_west[at : at + 2, :] = tracer[line, t, :2, :]


def stage_mail(own, west, east, mail):
    ny = own.shape[0] // 4
    for x in range(10):
        ref, at = (west, x) if x < 3 else (own, x - 3) if x < 7 else (east, x - 7)
        mail[pl.ds(x, ny, stride=10), :] = ref[at * ny : (at + 1) * ny, :]


def open_mail(mail, wet, own, east, west, state, up, down):
    ny, ntr, nx, depth = own.shape
    cells = ny * 10
    group = lax.broadcasted_iota(jnp.int32, (cells, depth), 1) // 32
    for f, at in ((0, 0), (1, 1), (2, 3), (3, 4)):
        field = None
        for s in range(4):
            turn = ((s - f) * 32) % depth
            part = mail[s]
            if turn:
                part = pltpu.roll(part, turn, 1)
            field = part if field is None else jnp.where(group == s, part, field)
        state[at * cells : (at + 1) * cells, :] = field
    state[2 * cells : 3 * cells, :] = wet[...]
    for j in range(4):
        for t in range(ntr):
            at = (j * ntr + t) * 4
            up[at : at + 4, :] = own[ny - 4 + j, t]
            down[at : at + 4, :] = own[j, t]
    base = 16 * ntr
    first = west.shape[0] - 8 * ntr
    for j in range(2):
        for t in range(ntr):
            at = base + (j * ntr + t) * 4
            low = first + (j * ntr + t) * 2
            high = low + 4 * ntr
            up[at : at + 2, :] = west[high : high + 2, :]
            up[at + 2 : at + 4, :] = east[high : high + 2, :]
            down[at : at + 2, :] = west[low : low + 2, :]
            down[at + 2 : at + 4, :] = east[low : low + 2, :]
    base = 24 * ntr
    for f in range(5):
        up[base + f * 30 : base + f * 30 + 30, :] = state[(f + 1) * cells - 30 : (f + 1) * cells, :]
        down[base + f * 30 : base + f * 30 + 30, :] = state[f * cells : f * cells + 30, :]


def unpack_levels(mail, temp, salt, east, north):
    nx, share, ny = temp.shape
    for x in range(nx):
        tall = mail[pl.ds(x, ny, stride=nx), :].T
        for f, ref in enumerate((temp, salt, east, north)):
            ref[x] = tall[f * share : (f + 1) * share]


def on_device(temp, salt, east, north, tracer, mask, bottom):
    nx, ny, ntr, levels = tracer.shape
    parts = lax.axis_size("gy")
    share = levels // parts
    span = parts * ny
    tracer = tracer.transpose(1, 2, 0, 3)

    deep = jnp.where(mask > 0, bottom, 0).astype(jnp.float32)
    stacked = jnp.stack([f.transpose(0, 2, 1) for f in (temp, salt, east, north)], axis=1)
    stacked = jnp.concatenate([stacked.reshape(nx * levels, span), deep], axis=0)
    side = (3 * span + nx + 8 * ntr, levels)
    own, to_east, to_west = call(
        pack_levels, [(nx * span, levels), side, side], stacked, tracer, name="pack_levels"
    )
    west_p = ring_send(to_east, "gx", 1)
    west_t = ring_send(tracer, "gx", 1)
    east_p = ring_send(to_west, "gx", -1)
    east_t = ring_send(tracer, "gx", -1)
    (mail,) = call(stage_mail, [(10 * span, levels)], own, west_p, east_p, name="stage_mail")
    mail = lax.all_to_all(
        mail.reshape(parts, 10 * ny, levels), "gy", split_axis=0, concat_axis=0, tiled=True
    )
    deep = jnp.concatenate(
        [west_p[3 * span + 1 : 3 * span + 4, :span], deep, east_p[3 * span : 3 * span + 3, :span]]
    )
    deep = lax.dynamic_slice_in_dim(deep, lax.axis_index("gy") * ny, ny, 1).T
    level = lax.broadcasted_iota(jnp.int32, (ny, 10, levels), 2).astype(jnp.float32)
    wet = (level < deep[:, :, None]).astype(jnp.float32).reshape(10 * ny, levels)
    y_rows = 24 * ntr + 150
    state, up, down = call(
        open_mail,
        [(50 * ny, levels), (y_rows, levels), (y_rows, levels)],
        mail,
        wet,
        tracer,
        east_p,
        west_p,
        name="open_mail",
    )
    south = ring_send(up, ROWS, 1)
    north = ring_send(down, ROWS, -1)
    inner = run_inner(tracer, east_t, west_t, state)
    tracer, mail = run_outer(tracer, east_t, west_t, south, north, state, *inner)
    mail = lax.all_to_all(mail, "gy", split_axis=0, concat_axis=0, tiled=True)
    fields = call(
        unpack_levels,
        [(nx, share, span)] * 4,
        mail.reshape(nx * span, levels),
        name="unpack_levels",
    )
    return (*[f.transpose(0, 2, 1) for f in fields], tracer.transpose(2, 0, 1, 3))


def solution(mesh):
    field = P("gx", "grp", "gy")
    tracers = P("gx", ("grp", "gy"), None, None)
    columns = P("gx", "grp")
    return jax.shard_map(
        on_device,
        mesh=mesh,
        in_specs=(field, field, field, field, tracers, columns, columns),
        out_specs=(field, field, field, field, tracers),
        check_vma=False,
    )
```

```python
import jax
import jax.numpy as jnp
from jax import lax
from jax.experimental import pallas as pl
from jax.experimental.pallas import tpu as pltpu
from jax.sharding import PartitionSpec as P

STEPS = 2
ADV_STEP = 0.1
DIFFUSION = 0.1
TURN_COS = 0.955336489125606
TURN_SIN = 0.29552020666134
PRESSURE = 0.2
HALINE = 0.8
BIO_STEP = 0.5
WATER_ATT = 0.005
CHLORO_ATT = 0.003
HEATING = 20.0
TEMP_RATE = 0.0633
NUTRIENT_HALF = 0.5
PREY_HALF = 0.5
GRAZING = 0.8
PHYTO_LOSS = 0.1
GRAZER_LOSS = 0.15
ASSIMILATE = 0.3
NTR = 17
ROWS = ("grp", "gy")


def ring_send(block, axis, step):
    names = axis if isinstance(axis, tuple) else (axis,)
    count = 1
    for name in names:
        count *= lax.axis_size(name)
    return lax.ppermute(block, axis, [(i, (i + step) % count) for i in range(count)])


def minmod(a, b):
    return jnp.maximum(jnp.minimum(a, b), 0.0) + jnp.minimum(jnp.maximum(a, b), 0.0)


def upwind(face, left, right):
    return face * jnp.where(face > 0, left, right)


def physics_rows(get, rows, put_west, put_east, put_south, put_mid):
    def buoy(row, shift):
        return get(0, row, shift) - HALINE * get(1, row, shift)

    def face_x(row, shift):
        gate = get(2, row, shift) * get(2, row, shift + 1)
        turned = TURN_COS * get(3, row, shift) + TURN_SIN * get(4, row, shift)
        return gate * (turned - PRESSURE * (buoy(row, shift + 1) - buoy(row, shift)))

    def face_y(row):
        gate = get(2, row, 0) * get(2, row + 1, 0)
        turned = TURN_COS * get(4, row, 0) - TURN_SIN * get(3, row, 0)
        return gate * (turned - PRESSURE * (buoy(row + 1, 0) - buoy(row, 0)))

    def body(row, carry):
        put_west(row, face_x(row, -1))
        put_east(row, face_x(row, 0))
        put_south(row, face_y(row - 1))
        wet = get(2, row, 0)
        open_e, open_w = wet * get(2, row, 1), wet * get(2, row, -1)
        open_n, open_s = wet * get(2, row + 1, 0), wet * get(2, row - 1, 0)
        fresh = []
        for f in (0, 1):
            q = get(f, row, 0)
            lap = (
                open_e * (get(f, row, 1) - q)
                - open_w * (q - get(f, row, -1))
                + open_n * (get(f, row + 1, 0) - q)
                - open_s * (q - get(f, row - 1, 0))
            )
            fresh.append(wet * (q + DIFFUSION * lap))
        put_mid(row, *fresh)
        return carry

    lax.fori_loop(0, rows, body, 0, unroll=True)
    put_south(rows, face_y(rows - 1))


def advect_all(read, dst, width, rows, west, east, south):
    def body(t, carry):
        def cell(e, shift=0):
            return read(e, t, 2 + shift)

        below, here = cell(1), cell(2)
        d_low = here - below
        left_y = below + 0.5 * minmod(below - cell(0), d_low)
        flux_prev = None
        change_x = None
        q_prev = None
        for e in range(2, rows + 3):
            above = cell(e + 1)
            d_high = above - here
            half = 0.5 * minmod(d_low, d_high)
            flux = upwind(south[e - 2, :width, :], left_y, here - half)
            if flux_prev is not None:
                dst[e - 3, t, :width, :] = q_prev - ADV_STEP * (change_x + (flux - flux_prev))
            if e < rows + 2:
                m2, m1, p1, p2 = cell(e, -2), cell(e, -1), cell(e, 1), cell(e, 2)
                d0, d1, d2, d3 = m1 - m2, here - m1, p1 - here, p2 - p1
                h_m, h_0, h_p = 0.5 * minmod(d0, d1), 0.5 * minmod(d1, d2), 0.5 * minmod(d2, d3)
                change_x = upwind(east[e - 2, :width, :], here + h_0, p1 - h_p) - upwind(
                    west[e - 2, :width, :], m1 + h_m, here - h_0
                )
            flux_prev, q_prev = flux, here
            left_y = here + half
            here, d_low = above, d_high
        return carry

    lax.fori_loop(0, NTR, body, 0)


def absorb_rows(cells, width, rows, absorb):
    def body(row, carry):
        chloro = 0.3 * cells[row, 1, :width, :]
        for c in range(1, 8):
            chloro = chloro + (0.3 + 0.1 * c) * cells[row, 1 + c, :width, :]
        absorb[row, :, :] = WATER_ATT + CHLORO_ATT * jnp.abs(chloro)
        return carry

    lax.fori_loop(0, rows, body, 0, unroll=True)


def dim_light(absorb, light, rows, width):
    depth = absorb.shape[-1]
    above = lax.broadcasted_iota(jnp.int32, (depth, depth), 0)
    level = lax.broadcasted_iota(jnp.int32, (depth, depth), 1)
    upper = jnp.where(above < level, 1.0, jnp.where(above == level, 0.5, 0.0))
    optical = jnp.dot(
        absorb[...].reshape(rows * width, depth),
        upper.astype(jnp.float32),
        precision=lax.Precision.HIGHEST,
        preferred_element_type=jnp.float32,
    )
    light[...] = jnp.exp(-optical).reshape(rows, width, depth)


def react_rows(cells, width, rows, absorb, light, halfway, wetness, put_temp):
    def body(row, carry):
        lit = light[row]
        wet = wetness(row)
        mid = halfway(row)
        nutrient = cells[row, 0, :width, :]
        drive = jnp.exp(TEMP_RATE * mid) * (nutrient / (jnp.abs(nutrient) + NUTRIENT_HALF)) * lit
        change = jnp.zeros_like(nutrient)
        for c in range(8):
            p = cells[row, 1 + c, :width, :]
            z = cells[row, 9 + c, :width, :]
            growth = (0.6 + 0.15 * c) * drive / (lit + (0.1 + 0.1 * c)) * p
            grazed = GRAZING * z * p / (jnp.abs(p) + PREY_HALF)
            change = change + (
                PHYTO_LOSS * p + GRAZER_LOSS * z + (1.0 - ASSIMILATE) * grazed - growth
            )
            cells[row, 1 + c, :width, :] = wet * (
                p + BIO_STEP * (growth - grazed - PHYTO_LOSS * p)
            )
            cells[row, 9 + c, :width, :] = wet * (
                z + BIO_STEP * (ASSIMILATE * grazed - GRAZER_LOSS * z)
            )
        cells[row, 0, :width, :] = wet * (nutrient + BIO_STEP * change)
        put_temp(row, mid + HEATING * absorb[row] * lit * wet)
        return carry

    lax.fori_loop(0, rows, body, 0, unroll=True)


def store_rows(ref):
    def put(row, value):
        ref[row] = value

    return put


def inner_rows(
    own, east, west, state,
    cells, u_east, v_south, mid,
    src, u_west, absorb, light,
):
    ny, ntr, nx, depth = own.shape
    rows = ny - 4

    def place(y, carry):
        src[y, :, 0:4, :] = west[y]
        src[y, :, 4:8, :] = own[y]
        src[y, :, 8:12, :] = east[y]
        return carry

    lax.fori_loop(0, ny, place, 0)

    def get(f, row, shift):
        return state[pl.ds((f * ny + row + 2) * 10 + 1 + shift, 8), :]

    def put_mid(row, temp, salt):
        mid[0, row] = temp
        mid[1, row] = salt

    def put_temp(row, value):
        mid[0, row] = value

    physics_rows(
        get, rows, store_rows(u_west), store_rows(u_east), store_rows(v_south), put_mid
    )
    advect_all(lambda e, t, x: src[e, t, x : x + 8, :], cells, 8, rows, u_west, u_east, v_south)
    absorb_rows(cells, 8, rows, absorb)
    dim_light(absorb, light, rows, 8)
    react_rows(
        cells, 8, rows, absorb, light, lambda row: mid[0, row], lambda row: get(2, row, 0), put_temp
    )


def outer_rows(
    own, east, west, south_in, north_in, state, cells_in, u_in, v_in, mid_in,
    out, mail,
    src, phys, wets, u_west, u_east, v_south, mid, edge, absorb, light,
    u_west2, u_east2, v_south2, mid2, absorb2, light2, fields,
):
    ny, ntr, nx, depth = own.shape
    inner = ny - 4

    def place(y, carry):
        for k, top, at in ((0, 0, 4), (1, ny - 4, 0)):
            src[k, y + at, :, 0:4, :] = west[top + y]
            src[k, y + at, :, 4:8, :] = own[top + y]
            src[k, y + at, :, 8:12, :] = east[top + y]
        return carry

    lax.fori_loop(0, 4, place, 0)
    wing = 4 * ntr * nx

    def place_rows(t, carry):
        for j in range(4):
            at = pl.multiple_of((j * ntr + t) * 4, 4)
            src[0, j, t, 4:8, :] = south_in[pl.ds(at, 4), :]
            src[1, 4 + j, t, 4:8, :] = north_in[pl.ds(at, 4), :]
        for j in range(2):
            at = wing + (j * ntr + t) * 4
            src[0, 2 + j, t, 2:4, :] = south_in[pl.ds(at, 2), :]
            src[0, 2 + j, t, 8:10, :] = south_in[pl.ds(at + 2, 2), :]
            src[1, 4 + j, t, 2:4, :] = north_in[pl.ds(at, 2), :]
            src[1, 4 + j, t, 8:10, :] = north_in[pl.ds(at + 2, 2), :]
        return carry

    lax.fori_loop(0, ntr, place_rows, 0)
    for f in range(5):
        for j in range(3):
            at = wing + wing // 2 + (f * 3 + j) * 10
            low, high = (f * ny + j) * 10, (f * ny + ny - 3 + j) * 10
            phys[0, f, j, 0:10, :] = south_in[at : at + 10, :]
            phys[0, f, 3 + j, 0:10, :] = state[low : low + 10, :]
            phys[1, f, j, 0:10, :] = state[high : high + 10, :]
            phys[1, f, 3 + j, 0:10, :] = north_in[at : at + 10, :]
    wets[0] = phys[0, 2, 2]
    wets[ny + 1] = phys[1, 2, 3]
    for y in range(ny):
        at = (2 * ny + y) * 10
        wets[y + 1, 0:10, :] = state[at : at + 10, :]
    for y in range(inner):
        mid[0, 4 + y] = mid_in[0, y]
        mid[1, 4 + y] = mid_in[1, y]
        u_east[4 + y] = u_in[y]
        v_south[4 + y] = v_in[y]

    for k, at in ((0, 0), (1, inner + 4)):

        def get(f, row, shift):
            return phys[k, f, row + 1, 1 + shift : 9 + shift, :]

        def put_mid(row, temp, salt):
            mid[0, at + row] = temp
            mid[1, at + row] = salt

        here = pl.ds(at, 4)
        faces = v_south.at[pl.ds(at, 5)]
        physics_rows(
            get,
            4,
            store_rows(u_west.at[pl.ds(4 * k, 4)]),
            store_rows(u_east.at[here]),
            store_rows(faces),
            put_mid,
        )
        advect_all(
            lambda e, t, x: src[k, e, t, x : x + 8, :],
            edge.at[k],
            8,
            4,
            u_west.at[pl.ds(4 * k, 4)],
            u_east.at[here],
            faces,
        )
        absorb_rows(edge.at[k], 8, 4, absorb.at[pl.ds(4 * k, 4)])
    dim_light(absorb, light, 8, 8)
    for k, at in ((0, 0), (1, inner + 4)):

        def put_temp(row, value):
            mid[0, at + row] = value

        react_rows(
            edge.at[k],
            8,
            4,
            absorb.at[pl.ds(4 * k, 4)],
            light.at[pl.ds(4 * k, 4)],
            lambda row: mid[0, at + row],
            lambda row: phys[k, 2, row + 1, 1:9, :],
            put_temp,
        )

    def get2(f, row, shift):
        cut = slice(2 + shift, 6 + shift)
        if f < 2:
            return mid[f, row + 2, cut, :]
        if f == 2:
            return wets[row + 1, 3 + shift : 7 + shift, :]
        if f == 3:
            return u_east[row + 2, cut, :]
        return v_south[row + 3, cut, :]

    def read2(e, t, x):
        if e < 4:
            return edge[0, e, t, x : x + 4, :]
        if e < inner + 4:
            return cells_in[e - 4, t, x : x + 4, :]
        return edge[1, e - inner - 4, t, x : x + 4, :]

    def put_mid2(row, temp, salt):
        mid2[row] = temp
        fields[1, pl.ds(row * 4, 4), :] = salt

    def put_east2(row, value):
        u_east2[row] = value
        fields[2, pl.ds(row * 4, 4), :] = value

    physics_rows(get2, ny, store_rows(u_west2), put_east2, store_rows(v_south2), put_mid2)
    advect_all(read2, out, 4, ny, u_west2, u_east2, v_south2)
    absorb_rows(out, 4, ny, absorb2)
    dim_light(absorb2, light2, ny, 4)

    def put_temp2(row, value):
        fields[0, pl.ds(row * 4, 4), :] = value
        fields[3, pl.ds(row * 4, 4), :] = v_south2[row + 1]

    react_rows(
        out, 4, ny, absorb2, light2, lambda row: mid2[row], lambda row: get2(2, row, 0), put_temp2
    )

    group = lax.broadcasted_iota(jnp.int32, (4 * ny, depth), 1) // 32
    for g in range(4):
        packed = None
        for f in range(4):
            turn = ((f - g) * 32) % depth
            part = fields[f]
            if turn:
                part = pltpu.roll(part, turn, 1)
            packed = part if packed is None else jnp.where(group == f, part, packed)
        mail[g] = packed


def run_inner(own, east, west, state):
    ny, ntr, nx, depth = own.shape
    rows = ny - 4
    return call(
        inner_rows,
        [(rows, ntr, 8, depth), (rows, 8, depth), (rows + 1, 8, depth), (2, rows, 8, depth)],
        own,
        east,
        west,
        state,
        name="inner_rows",
        scratch=[
            (ny, ntr, 16, depth),
            (rows, 8, depth),
            (rows, 8, depth),
            (rows, 8, depth),
        ],
    )


def run_outer(own, east, west, south, north, state, *inner):
    ny, ntr, nx, depth = own.shape
    ry = ny + 4
    return call(
        outer_rows,
        [(ny, ntr, nx, depth), (4, ny * nx, depth)],
        own,
        east,
        west,
        south,
        north,
        state,
        *inner,
        name="outer_rows",
        scratch=[
            (2, 8, ntr, 16, depth),
            (2, 5, 6, 16, depth),
            (ny + 2, 16, depth),
            (8, 8, depth),
            (ry, 8, depth),
            (ry + 1, 8, depth),
            (2, ry, 8, depth),
            (2, 4, ntr, 8, depth),
            (8, 8, depth),
            (8, 8, depth),
            (ny, nx, depth),
            (ny, nx, depth),
            (ny + 1, nx, depth),
            (ny, nx, depth),
            (ny, nx, depth),
            (ny, nx, depth),
            (4, ny * nx, depth),
        ],
    )


def call(body, out_shapes, *args, name, scratch=()):
    whole = pl.BlockSpec(memory_space=pltpu.VMEM)
    return pl.pallas_call(
        body,
        out_shape=tuple(jax.ShapeDtypeStruct(s, jnp.float32) for s in out_shapes),
        in_specs=[whole] * len(args),
        out_specs=(whole,) * len(out_shapes),
        scratch_shapes=[pltpu.VMEM(shape, jnp.float32) for shape in scratch],
        compiler_params=pltpu.CompilerParams(vmem_limit_bytes=40 * 1024 * 1024),
        name=name,
    )(*args)


def pack_levels(stacked, tracer, own, to_east, to_west):
    span = stacked.shape[1]
    depth = own.shape[1]
    nx = own.shape[0] // span
    for x in range(nx):
        rows = stacked[x * depth : (x + 1) * depth, :].T
        own[x * span : (x + 1) * span, :] = rows
        if x > 0:
            to_east[(x - 1) * span : x * span, :] = rows
        if x < nx - 1:
            to_west[x * span : (x + 1) * span, :] = rows
    for ref in (to_east, to_west):
        ref[3 * span : 3 * span + nx, :] = jnp.zeros((nx, depth), jnp.float32)
        ref[3 * span : 3 * span + nx, 0:span] = stacked[nx * depth :, :]
    ny, ntr = tracer.shape[:2]
    base = 3 * span + nx
    for k, line in enumerate((0, 1, ny - 2, ny - 1)):
        for t in range(ntr):
            at = base + (k * ntr + t) * 2
            to_east[at : at + 2, :] = tracer[line, t, nx - 2 :, :]
            to_west[at : at + 2, :] = tracer[line, t, :2, :]


def stage_mail(own, west, east, mail):
    ny = own.shape[0] // 4
    for x in range(10):
        ref, at = (west, x) if x < 3 else (own, x - 3) if x < 7 else (east, x - 7)
        mail[pl.ds(x, ny, stride=10), :] = ref[at * ny : (at + 1) * ny, :]


def open_mail(mail, wet, own, east, west, state, up, down):
    ny, ntr, nx, depth = own.shape
    cells = ny * 10
    group = lax.broadcasted_iota(jnp.int32, (cells, depth), 1) // 32
    for f, at in ((0, 0), (1, 1), (2, 3), (3, 4)):
        field = None
        for s in range(4):
            turn = ((s - f) * 32) % depth
            part = mail[s]
            if turn:
                part = pltpu.roll(part, turn, 1)
            field = part if field is None else jnp.where(group == s, part, field)
        state[at * cells : (at + 1) * cells, :] = field
    state[2 * cells : 3 * cells, :] = wet[...]
    for j in range(4):
        for t in range(ntr):
            at = (j * ntr + t) * 4
            up[at : at + 4, :] = own[ny - 4 + j, t]
            down[at : at + 4, :] = own[j, t]
    base = 16 * ntr
    first = west.shape[0] - 8 * ntr
    for j in range(2):
        for t in range(ntr):
            at = base + (j * ntr + t) * 4
            low = first + (j * ntr + t) * 2
            high = low + 4 * ntr
            up[at : at + 2, :] = west[high : high + 2, :]
            up[at + 2 : at + 4, :] = east[high : high + 2, :]
            down[at : at + 2, :] = west[low : low + 2, :]
            down[at + 2 : at + 4, :] = east[low : low + 2, :]
    base = 24 * ntr
    for f in range(5):
        up[base + f * 30 : base + f * 30 + 30, :] = state[(f + 1) * cells - 30 : (f + 1) * cells, :]
        down[base + f * 30 : base + f * 30 + 30, :] = state[f * cells : f * cells + 30, :]


def unpack_levels(mail, temp, salt, east, north):
    nx, share, ny = temp.shape
    for x in range(nx):
        tall = mail[pl.ds(x, ny, stride=nx), :].T
        for f, ref in enumerate((temp, salt, east, north)):
            ref[x] = tall[f * share : (f + 1) * share]


def on_device(temp, salt, east, north, tracer, mask, bottom):
    nx, ny, ntr, levels = tracer.shape
    parts = lax.axis_size("gy")
    share = levels // parts
    span = parts * ny
    tracer = tracer.transpose(1, 2, 0, 3)

    deep = jnp.where(mask > 0, bottom, 0).astype(jnp.float32)
    stacked = jnp.stack([f.transpose(0, 2, 1) for f in (temp, salt, east, north)], axis=1)
    stacked = jnp.concatenate([stacked.reshape(nx * levels, span), deep], axis=0)
    side = (3 * span + nx + 8 * ntr, levels)
    own, to_east, to_west = call(
        pack_levels, [(nx * span, levels), side, side], stacked, tracer, name="pack_levels"
    )
    west_p = ring_send(to_east, "gx", 1)
    west_t = ring_send(tracer, "gx", 1)
    east_p = ring_send(to_west, "gx", -1)
    east_t = ring_send(tracer, "gx", -1)
    (mail,) = call(stage_mail, [(10 * span, levels)], own, west_p, east_p, name="stage_mail")
    mail = lax.all_to_all(
        mail.reshape(parts, 10 * ny, levels), "gy", split_axis=0, concat_axis=0, tiled=True
    )
    deep = jnp.concatenate(
        [west_p[3 * span + 1 : 3 * span + 4, :span], deep, east_p[3 * span : 3 * span + 3, :span]]
    )
    deep = lax.dynamic_slice_in_dim(deep, lax.axis_index("gy") * ny, ny, 1).T
    level = lax.broadcasted_iota(jnp.int32, (ny, 10, levels), 2).astype(jnp.float32)
    wet = (level < deep[:, :, None]).astype(jnp.float32).reshape(10 * ny, levels)
    y_rows = 24 * ntr + 150
    state, up, down = call(
        open_mail,
        [(50 * ny, levels), (y_rows, levels), (y_rows, levels)],
        mail,
        wet,
        tracer,
        east_p,
        west_p,
        name="open_mail",
    )
    south = ring_send(up, ROWS, 1)
    north = ring_send(down, ROWS, -1)
    inner = run_inner(tracer, east_t, west_t, state)
    tracer, mail = run_outer(tracer, east_t, west_t, south, north, state, *inner)
    mail = lax.all_to_all(mail, "gy", split_axis=0, concat_axis=0, tiled=True)
    fields = call(
        unpack_levels,
        [(nx, share, span)] * 4,
        mail.reshape(nx * span, levels),
        name="unpack_levels",
    )
    return (*[f.transpose(0, 2, 1) for f in fields], tracer.transpose(2, 0, 1, 3))


def solution(mesh):
    field = P("gx", "grp", "gy")
    tracers = P("gx", ("grp", "gy"), None, None)
    columns = P("gx", "grp")
    return jax.shard_map(
        on_device,
        mesh=mesh,
        in_specs=(field, field, field, field, tracers, columns, columns),
        out_specs=(field, field, field, field, tracers),
        check_vma=False,
    )
```
